512 devices in a mesh: slab: 128 (over y, z, core), sub: 4 (over x).
Axes of the slice: x: 4, y: 4, z: 16, core: 2. Of those that a mesh axis runs over, the one named last changes fastest.
Arguments:
- mode_shapes: bfloat16 [32, 6, 1024, 512], P(None, None, 'slab', 'sub')
- span_stiff: float32 [6, 1024, 512], P(None, 'slab', 'sub'), may hold values from -4 to 4
- chord_stiff: float32 [6, 1024, 512], P(None, 'slab', 'sub'), may hold values from -4 to 4
- span_geo: float32 [1024, 512], P('slab', 'sub'), may hold values from 0.2 to 2
- chord_geo: float32 [1024, 512], P('slab', 'sub'), may hold values from 0.2 to 2
- ground: float32 [6, 1024, 512], P(None, 'slab', 'sub'), may hold values from 0.2 to 2
- chord_len: int32 [1024], replicated, may hold values from 192 to 512, as said below
Outputs:
- adjoint: float32 [32, 6, 1024, 512], P(None, None, 'slab', 'sub')
- residual: float32 [32, 6, 1024, 512], P(None, None, 'slab', 'sub')
The draws below stay inside these ranges and needn't reach their ends.
Inputs may be any that keep to these rules, and one draw needn't show every extreme that they name: chord_len[0] = 512.
All inputs are finite; a program needn't handle non-finite values.
Results may differ from the reference program's by a relative error of at most 0.0003.
Values sent between devices are 32-bit elements; how exact they have to be, the bound alone decides.
A program may use at most 64 MiB of HBM per device.

```python
import math
import jax
import jax.numpy as jnp
from jax import lax

MODES = 32
DOF = 6
ITERS = 2
NS = 1024
NC = 512


def draw_mode_shapes(key, part):
    first_key = jax.random.fold_in(key, 0)
    shape_full = (MODES, DOF, NS, NC)
    station = jnp.arange(NS, dtype=jnp.float32) / NS
    amplitude = (0.3 * (0.5 + 1.5 * station))[None, None, :, None]
    values = jnp.clip(jax.random.normal(first_key, shape_full, jnp.float32), -4.0, 4.0)
    return (values * amplitude).astype(jnp.bfloat16)


def draw_chord_len(key, part):
    stations = jnp.arange(NS, dtype=jnp.int32)
    taper = NC // 2 * stations // NS
    jitter = jax.random.randint(key, (NS,), 0, max(NC // 8, 1), dtype=jnp.int32)
    jitter = jnp.where(stations == 0, 0, jitter)
    return (NC - taper - jitter).astype(jnp.int32)


def levels(stream_key, shape, shards, low, top_value):
    factor_of, own = 1.0, jax.random.fold_in(stream_key, 6)
    for dim, blocks in shards:
        heights = jnp.exp(jax.random.uniform(jax.random.fold_in(own, dim), (blocks,), jnp.float32, low / len(shards), top_value / len(shards)))
        factor_of = factor_of * jnp.repeat(heights, shape[dim] // blocks).reshape([-1 if axis == dim else 1 for axis in range(len(shape))])
    return factor_of


def bell_draw(key, extent, spread, bound, cuts=(), kind=jnp.bfloat16):
    values = jax.random.normal(key, extent, jnp.float32) * spread
    if len(cuts) > 0:
        values = levels(key, extent, cuts, -0.22, 0.18) * values
    return jnp.clip(values, min=-bound, max=bound).astype(kind)


def setup_inputs(seed: int = 0) -> dict:
    streams_of = jax.random.split(jax.random.key(seed), 8)
    mode_shapes = draw_mode_shapes(jax.random.fold_in(streams_of[7], 71), 0)
    span_stiff = bell_draw(streams_of[1], (DOF, NS, NC), 0.7, 4.0, ((1, 128), (2, 4)), jnp.float32)
    chord_stiff = bell_draw(streams_of[2], (DOF, NS, NC), 0.7, 4.0, ((1, 128), (2, 4)), jnp.float32)
    span_geo = jnp.clip(jnp.exp(math.log(2.0) - 2.3025851 * jax.random.uniform(streams_of[3], (NS, NC), jnp.float32) ** levels(streams_of[3], (NS, NC), ((0, 128), (1, 4)), -0.2, 0.2)), 0.2, 2.0)
    chord_geo = jnp.clip(jnp.exp(math.log(2.0) - 2.3025851 * jax.random.uniform(streams_of[4], (NS, NC), jnp.float32) ** levels(streams_of[4], (NS, NC), ((0, 128), (1, 4)), -0.2, 0.2)), 0.2, 2.0)
    ground = jnp.clip(jnp.exp(math.log(2.0) - 2.3025851 * jax.random.uniform(streams_of[5], (DOF, NS, NC), jnp.float32) ** levels(streams_of[5], (DOF, NS, NC), ((1, 128), (2, 4)), -0.2, 0.2)), 0.2, 2.0)
    chord_len = draw_chord_len(jax.random.fold_in(streams_of[7], 71), 0)
    return dict(mode_shapes=mode_shapes, span_stiff=span_stiff, chord_stiff=chord_stiff, span_geo=span_geo, chord_geo=chord_geo, ground=ground, chord_len=chord_len)


def ahead_of(field, along):
    remainder = lax.slice_in_dim(field, 1, field.shape[along], axis=along)
    zero_rim = jnp.zeros_like(lax.slice_in_dim(field, 0, 1, axis=along))
    return jnp.concatenate([remainder, zero_rim], axis=along)

def behind_of(field, along):
    remainder = lax.slice_in_dim(field, 0, field.shape[along] - 1, axis=along)
    zero_rim = jnp.zeros_like(lax.slice_in_dim(field, 0, 1, axis=along))
    return jnp.concatenate([zero_rim, remainder], axis=along)

def edge_masks(chord_len):
    columns = jnp.arange(NC, dtype=jnp.int32)[None, :]
    length_here = chord_len[:, None]
    length_next = jnp.concatenate([chord_len[1:], jnp.zeros((1,), jnp.int32)])[:, None]
    span_live = ((columns < length_here) & (columns < length_next)).astype(jnp.float32)
    chord_live = (columns + 1 < length_here).astype(jnp.float32)
    return (span_live, chord_live)

def node_blocks(span_stiff, chord_stiff, span_live, chord_live, ground):
    count = ground.shape[0]
    blocks = []
    for i in range(count):
        block_row = []
        for j in range(count):
            span_pair = span_stiff[i] * span_stiff[j] * span_live
            chord_pair = chord_stiff[i] * chord_stiff[j] * chord_live
            entry = span_pair + behind_of(span_pair, 0) + chord_pair + behind_of(chord_pair, 1)
            if i == j:
                entry = entry + ground[i]
            block_row.append(entry)
        blocks.append(block_row)
    return blocks

def factor_blocks(blocks):
    count = len(blocks)
    factor = [[None] * count for i in range(count)]
    inverse = [None] * count
    for j in range(count):
        running = blocks[j][j]
        for k in range(j):
            running = running - factor[j][k] * factor[j][k]
        diag_root = jnp.sqrt(running)
        factor[j][j] = diag_root
        inverse[j] = 1.0 / diag_root
        for i in range(j + 1, count):
            running = blocks[i][j]
            for k in range(j):
                running = running - factor[i][k] * factor[j][k]
            factor[i][j] = running * inverse[j]
    return (factor, inverse)

def solve_blocks(factor, inverse, vector):
    count = len(inverse)
    forward = []
    for i in range(count):
        running = vector[:, i]
        for j in range(i):
            running = running - factor[i][j][None] * forward[j]
        forward.append(running * inverse[i][None])
    backward = [None] * count
    for i in reversed(range(count)):
        running = forward[i]
        for j in range(i + 1, count):
            running = running - factor[j][i][None] * backward[j]
        backward[i] = running * inverse[i][None]
    return jnp.stack(backward, axis=1)

def operate(field, span_stiff, chord_stiff, span_live, chord_live, ground):
    result = ground[None] * field
    for stiffness, live_mask, along in ((span_stiff, span_live, 2), (chord_stiff, chord_live, 3)):
        strain = lax.optimization_barrier(jnp.sum(stiffness[None] * (ahead_of(field, along) - field), axis=1)) * live_mask[None]
        forces = stiffness[None] * strain[:, None]
        result = result - forces + behind_of(forces, along)
    return result

def loads(mode_field, span_stiff, chord_stiff, span_geo, chord_geo, span_live, chord_live):
    result = jnp.zeros_like(mode_field)
    for stiffness, geometric, live_mask, along in ((span_stiff, span_geo, span_live, 2), (chord_stiff, chord_geo, chord_live, 3)):
        jump = ahead_of(mode_field, along) - mode_field
        weight = lax.optimization_barrier(jnp.sum(jump * jump, axis=1)) * (geometric * live_mask)[None]
        forces = stiffness[None] * weight[:, None]
        result = result - forces + behind_of(forces, along)
    return result

def reference(mode_shapes, span_stiff, chord_stiff, span_geo, chord_geo, ground, chord_len):
    mode_field = mode_shapes.astype(jnp.float32)
    span_live, chord_live = edge_masks(chord_len)
    factor, inverse = factor_blocks(node_blocks(span_stiff, chord_stiff, span_live, chord_live, ground))
    load = loads(mode_field, span_stiff, chord_stiff, span_geo, chord_geo, span_live, chord_live)
    solution = jnp.zeros_like(load)
    residual = load
    precond = solve_blocks(factor, inverse, residual)
    direction = precond
    precond_norm = lax.optimization_barrier(jnp.sum(residual * precond, axis=(1, 2, 3)))
    for step in range(ITERS):
        image = operate(direction, span_stiff, chord_stiff, span_live, chord_live, ground)
        step_size = precond_norm / lax.optimization_barrier(jnp.sum(direction * image, axis=(1, 2, 3)))
        solution = solution + step_size[:, None, None, None] * direction
        residual = residual - step_size[:, None, None, None] * image
        if step + 1 < ITERS:
            precond = solve_blocks(factor, inverse, residual)
            norm_next = lax.optimization_barrier(jnp.sum(residual * precond, axis=(1, 2, 3)))
            direction = precond + (norm_next / precond_norm)[:, None, None, None] * direction
            precond_norm = norm_next
    return (solution, residual)
```

```python
import functools

import jax
import jax.numpy as jnp
from jax import lax
from jax.experimental import pallas as pl
from jax.experimental.pallas import tpu as pltpu
from jax.sharding import PartitionSpec as P

MESH = pl.DeviceIdType.MESH
D = 6
R, C = 8, 128
M = 32
GROUPS = 4
GM = M // GROUPS
UNROLL = 2


def digit_stages(n_slab, n_sub):
    core = 2
    z = 16 if n_slab % 32 == 0 else 1
    y = n_slab // (core * z)
    stages = [[("slab", 1, core), ("sub", 1, n_sub)]]
    if z > 1:
        stages.append([("slab", core, z)])
    if y > 1:
        stages.append([("slab", core * z, y)])
    return stages


def stage_partners(digits, slab, sub):
    total = 1
    for _, _, size in digits:
        total *= size
    partners = []
    for offset in range(1, total):
        rest, at = offset, {"slab": slab, "sub": sub}
        for axis, stride, size in digits:
            step, rest = rest % size, rest // size
            digit = (at[axis] // stride) % size
            at[axis] = at[axis] + ((digit + step) % size - digit) * stride
        partners.append((at["slab"], at["sub"]))
    return partners


def total_of(terms):
    terms = list(terms)
    while len(terms) > 1:
        terms = [sum(terms[i : i + 2][1:], terms[i]) for i in range(0, len(terms), 2)]
    return terms[0]


def kernel(
    n_slab,
    n_sub,
    stages,
    m_any,
    ss_any,
    cs_any,
    sg_any,
    cg_any,
    gr_any,
    len_any,
    x_ref,
    r_ref,
    len_ref,
    m_in,
    ss,
    cs,
    sg,
    cg,
    gr,
    field,
    r0,
    z0,
    q0,
    d0,
    ssb,
    csb,
    fac,
    ts,
    us,
    tc,
    uc,
    prod,
    flip,
    coef_send,
    coef_span,
    coef_chord,
    row_first,
    row_last,
    from_ahead,
    from_behind,
    col_own,
    col_ahead,
    col_behind,
    w_ahead,
    w_behind,
    w_col,
    t_send,
    u_send,
    u_ahead,
    t_behind,
    tu_send,
    tu_ahead,
    tu_behind,
    *rest,
):
    parts = rest[: len(stages)]
    in_sem, send_sem, recv_sem = rest[len(stages) :]
    slab, sub = lax.axis_index("slab"), lax.axis_index("sub")
    ahead = (lax.rem(slab + 1, n_slab), sub)
    behind = (lax.rem(slab + n_slab - 1, n_slab), sub)
    right = (slab, lax.rem(sub + 1, n_sub))
    left = (slab, lax.rem(sub + n_sub - 1, n_sub))
    partners = [stage_partners(digits, slab, sub) for digits in stages]

    loads = []
    for k, (source, target) in enumerate(
        ((m_any, m_in), (ss_any, ss), (cs_any, cs), (sg_any, sg), (cg_any, cg), (gr_any, gr), (len_any, len_ref))
    ):
        copy = pltpu.make_async_copy(source, target, in_sem.at[k])
        copy.start()
        loads.append(copy)

    barrier = pltpu.get_barrier_semaphore()
    greeted = [ahead, behind, right, left] + [p for group in partners for p in group]
    for device in greeted:
        pl.semaphore_signal(barrier, inc=1, device_id=device, device_id_type=MESH)

    row = lax.broadcasted_iota(jnp.int32, (R, C), 0)
    lane = lax.broadcasted_iota(jnp.int32, (R, C), 1)
    pair = lax.shift_right_logical(lane, 1)
    even = lane - 2 * pair == 0

    def tile(k):
        return pl.ds(pl.multiple_of(k * R, R), R)

    def wide(value):
        return jnp.broadcast_to(value, (R, C))

    sent = []
    count = [0]

    def send(source, target, device):
        k = count[0]
        count[0] += 1
        copy = pltpu.make_async_remote_copy(
            src_ref=source,
            dst_ref=target,
            send_sem=send_sem.at[k],
            recv_sem=recv_sem.at[k],
            device_id=device,
            device_id_type=MESH,
        )
        copy.start()
        sent.append(copy)
        return copy

    loads[0].wait()

    def pack(i, packs):
        packs = list(packs)
        for u in range(UNROLL):
            j = i * UNROLL + u
            for c in range(D):
                value = m_in[j, c].astype(jnp.float32)
                field[tile(j * D + c), :] = value
                half = 32 * (c % 2)
                turned = pltpu.roll(value, 2 * (j + half) + 1, 1)
                packs[c // 2] = jnp.where(pair == j + half, turned, packs[c // 2])
        return tuple(packs)

    zero = jnp.zeros((R, C), jnp.float32)
    packs = lax.fori_loop(0, M // UNROLL, pack, (zero,) * 3)
    for v in range(3):
        col_own[pl.ds(v * R, R), :] = packs[v]
    for g in range(M // 8):
        for c in range(D):
            at = pl.ds((g * D + c) * 8, 8)
            row_first[at, :] = field[pl.ds((g * 8 * D + c) * R, 8, stride=D * R), :]
            row_last[at, :] = field[pl.ds((g * 8 * D + c) * R + R - 1, 8, stride=D * R), :]

    for copy in loads[1:]:
        copy.wait()
    span_coef, chord_coef = zero, zero
    for c in range(D + 1):
        mine = ss[c] if c < D else sg[...]
        span_coef = jnp.where(row == c, wide(mine[R - 1 :, :]), span_coef)
        mine = cs[c] if c < D else cg[...]
        chord_coef = jnp.where(lane == c, wide(mine[:, C - 1 :]), chord_coef)
    coef_send[0] = span_coef
    coef_send[1] = chord_coef

    pl.semaphore_wait(barrier, len(greeted))
    got_coef = [
        send(coef_send.at[0], coef_span, ahead),
        send(coef_send.at[1], coef_chord, right),
    ]
    got_cols = [send(col_own, col_behind, right), send(col_own, col_ahead, left)]
    got_rows = []
    for g in range(M // 8):
        at = pl.ds(g * 8 * D, 8 * D)
        got_rows.append(
            [
                send(row_last.at[at], from_behind.at[at], ahead),
                send(row_first.at[at], from_ahead.at[at], behind),
            ]
        )

    n_stations = n_slab * R
    first = slab * R
    length = jnp.zeros((R, C), jnp.int32)
    length_next = jnp.zeros((R, C), jnp.int32)
    length_prev = jnp.zeros((R, C), jnp.int32)
    for k in range(-1, R + 1):
        here = len_ref[jnp.clip(first + k, 0, n_stations - 1)]
        if 0 <= k < R:
            length = jnp.where(row == k, here, length)
        if k >= 1:
            length_next = jnp.where(row == k - 1, here, length_next)
        if k < R - 1:
            length_prev = jnp.where(row == k + 1, here, length_prev)
    column = lane + sub * C
    station = row + first
    one = jnp.ones((R, C), jnp.float32)
    span_live = jnp.where(
        (column < length) & (column < length_next) & (station < n_stations - 1), one, zero
    )
    span_live_b = jnp.where(
        (column < length) & (column < length_prev) & (station > 0), one, zero
    )
    chord_live = jnp.where(column + 1 < length, one, zero)
    chord_live_b = jnp.where((column < length) & (column > 0), one, zero)
    span_geo = sg[...] * span_live
    chord_geo = cg[...] * chord_live

    for copy in got_coef:
        copy.wait_recv()
    chord_ghost = coef_chord[...]
    for c in range(D):
        mine = ss[c]
        back = jnp.where(row == 0, wide(coef_span[pl.ds(c, 1), :]), pltpu.roll(mine, 1, 0))
        ssb[c] = back * span_live_b
        ss[c] = mine * span_live
        mine = cs[c]
        back = jnp.where(lane == 0, wide(chord_ghost[:, c : c + 1]), pltpu.roll(mine, 1, 1))
        csb[c] = back * chord_live_b
        cs[c] = mine * chord_live
    a_s = [ss[c] for c in range(D)]
    a_c = [cs[c] for c in range(D)]
    b_s = [ssb[c] for c in range(D)]
    b_c = [csb[c] for c in range(D)]
    low = [[None] * D for _ in range(D)]
    raw = [[None] * D for _ in range(D)]
    k = 0
    for j in range(D):
        for i in range(j, D):
            entry = (a_s[i] * a_s[j] + b_s[i] * b_s[j]) + (a_c[i] * a_c[j] + b_c[i] * b_c[j])
            if i == j:
                entry = entry + gr[i]
            for n in range(j):
                entry = entry - raw[i][n] * low[j][n]
            raw[i][j] = entry
        inverse = 1.0 / raw[j][j]
        fac[15 + j] = inverse
        for i in range(j + 1, D):
            low[i][j] = raw[i][j] * inverse
            fac[k] = low[i][j]
            k += 1

    def factors():
        low = {}
        k = 0
        for j in range(D):
            for i in range(j + 1, D):
                low[i, j] = fac[k]
                k += 1
        return low, [fac[15 + j] for j in range(D)]

    def solve(vector):
        low, inverse = factors()
        forward = []
        for i in range(D):
            running = vector[i]
            for j in range(i):
                running = running - low[i, j] * forward[j]
            forward.append(running)
        backward = [None] * D
        for i in reversed(range(D)):
            running = forward[i] * inverse[i]
            for j in range(i + 1, D):
                running = running - low[j, i] * backward[j]
            backward[i] = running
        return backward

    def dots(j, vector, packed):
        t_s = total_of(ss[c] * vector[c] for c in range(D))
        u_s = total_of(ssb[c] * vector[c] for c in range(D))
        t_c = total_of(cs[c] * vector[c] for c in range(D))
        u_c = total_of(csb[c] * vector[c] for c in range(D))
        ts[tile(j), :] = t_s
        us[tile(j), :] = u_s
        tc[tile(j), :] = t_c
        uc[tile(j), :] = u_c
        turned = pltpu.roll(jnp.where(lane == 0, u_c, t_c), 2 * j + 1, 1)
        return jnp.where(pair == j, turned, packed)

    def send_dots(turn, g, packed):
        at = pl.ds(turn * M + g * GM, GM)
        for b in range(GM // 8):
            from_mode = g * GM + b * 8
            to = pl.ds(turn * M + from_mode, 8)
            t_send[to, :] = ts[pl.ds(from_mode * R + R - 1, 8, stride=R), :]
            u_send[to, :] = us[pl.ds(from_mode * R, 8, stride=R), :]
        tu_send[turn, g] = packed
        return [
            send(t_send.at[at], t_behind.at[at], ahead),
            send(u_send.at[at], u_ahead.at[at], behind),
            send(tu_send.at[turn, g], tu_behind.at[turn, g], right),
            send(tu_send.at[turn, g], tu_ahead.at[turn, g], left),
        ]

    def edges_of(turn, g):
        return jnp.where(
            even,
            pltpu.roll(tu_ahead[turn, g], C - 1, 1),
            pltpu.roll(tu_behind[turn, g], 1, 1),
        )

    def operate(turn, j, vector, edge):
        t_s, u_s, t_c, u_c = ts[tile(j), :], us[tile(j), :], tc[tile(j), :], uc[tile(j), :]
        at = pl.ds(turn * M + j, 1)
        edge = pltpu.roll(edge, C - 1 - 2 * j, 1)
        u_s_next = jnp.where(row == R - 1, wide(u_ahead[at, :]), pltpu.roll(u_s, R - 1, 0))
        t_s_prev = jnp.where(row == 0, wide(t_behind[at, :]), pltpu.roll(t_s, 1, 0))
        u_c_next = jnp.where(lane == C - 1, edge, pltpu.roll(u_c, C - 1, 1))
        t_c_prev = jnp.where(lane == 0, edge, pltpu.roll(t_c, 1, 1))
        e_s, e_sb = u_s_next - t_s, u_s - t_s_prev
        e_c, e_cb = u_c_next - t_c, u_c - t_c_prev
        return [
            (gr[c] * vector[c] + (ssb[c] * e_sb - ss[c] * e_s)) + (csb[c] * e_cb - cs[c] * e_c)
            for c in range(D)
        ]

    def of_mode(ref, j):
        return [ref[tile(j * D + c), :] for c in range(D)]

    def keep(ref, j, vector):
        for c in range(D):
            ref[tile(j * D + c), :] = vector[c]

    def over_group(g, step, carry):
        def some(i, carry):
            for u in range(UNROLL):
                carry = step(g * GM + i * UNROLL + u, carry)
            return carry

        return lax.fori_loop(0, GM // UNROLL, some, carry)

    for copy in got_cols:
        copy.wait_recv()
    square = None
    for v in range(3):
        at = pl.ds(v * R, R)
        across = jnp.where(
            even, pltpu.roll(col_ahead[at, :], C - 1, 1), pltpu.roll(col_behind[at, :], 1, 1)
        )
        jump = across - col_own[at, :]
        square = jump * jump if square is None else square + jump * jump
    square = square + pltpu.roll(square, C // 2, 1)
    geo_b = chord_ghost[:, D : D + 1] * chord_live_b[:, :1]
    w_col[...] = square * jnp.where(even, wide(chord_geo[:, C - 1 :]), wide(geo_b))
    sg[...] = span_geo
    cg[...] = chord_geo
    geo_ahead = jnp.broadcast_to(span_geo[R - 1 :, :], (8, C))
    geo_behind = jnp.broadcast_to(coef_span[pl.ds(D, 1), :] * span_live_b[:1, :], (8, C))

    def load_step(j, packed):
        modes = of_mode(field, j)
        edge = pltpu.roll(w_col[...], C - 1 - 2 * j, 1)
        jumps = [pltpu.roll(value, R - 1, 0) - value for value in modes]
        w_s = total_of(jump * jump for jump in jumps) * sg[...]
        w_s = jnp.where(row == R - 1, wide(w_ahead[pl.ds(j, 1), :]), w_s)
        jumps = [pltpu.roll(value, C - 1, 1) - value for value in modes]
        w_c = total_of(jump * jump for jump in jumps) * cg[...]
        w_c = jnp.where(lane == C - 1, edge, w_c)
        w_sb = jnp.where(row == 0, wide(w_behind[pl.ds(j, 1), :]), pltpu.roll(w_s, 1, 0))
        w_cb = jnp.where(lane == 0, edge, pltpu.roll(w_c, 1, 1))
        load = [
            (ssb[c] * w_sb - ss[c] * w_s) + (csb[c] * w_cb - cs[c] * w_c) for c in range(D)
        ]
        first_z = solve(load)
        keep(r0, j, load)
        keep(z0, j, first_z)
        return dots(j, first_z, packed)

    got_first = []
    for g in range(GROUPS):
        for b in range(GM // 8):
            block = g * (GM // 8) + b
            for copy in got_rows[block]:
                copy.wait_recv()
            to_ahead, to_behind = [], []
            for c in range(D):
                at = pl.ds((block * D + c) * 8, 8)
                jump = from_ahead[at, :] - row_last[at, :]
                to_ahead.append(jump * jump)
                jump = row_first[at, :] - from_behind[at, :]
                to_behind.append(jump * jump)
            w_ahead[pl.ds(block * 8, 8), :] = total_of(to_ahead) * geo_ahead
            w_behind[pl.ds(block * 8, 8), :] = total_of(to_behind) * geo_behind
        got_first.append(send_dots(0, g, over_group(g, load_step, zero)))

    def first_step(edge, j, packed):
        z = of_mode(z0, j)
        image = operate(0, j, z, edge)
        left_over = [a - b for a, b in zip(of_mode(r0, j), image)]
        second = solve(left_over)
        keep(q0, j, image)
        keep(d0, j, second)
        prod[tile(j), :] = total_of(a * b for a, b in zip(z, image))
        prod[tile(M + j), :] = total_of(a * b for a, b in zip(z, left_over))
        prod[tile(2 * M + j), :] = total_of(a * b for a, b in zip(second, left_over))
        return dots(j, second, packed)

    got_second = []
    for g in range(GROUPS):
        for copy in got_first[g]:
            copy.wait_recv()
        edge = edges_of(0, g)
        packed = over_group(g, functools.partial(first_step, edge), zero)
        got_second.append(send_dots(1, g, packed))

    def fold(k):
        rows = [prod[pl.ds(k * 8 * R + n, 8, stride=R), :] for n in range(R)]
        flip[pl.ds(k * 8, 8), :] = total_of(rows)

    for k in range(3 * M // 8):
        fold(k)

    def second_step(edge, j, carry):
        second = of_mode(d0, j)
        image = operate(1, j, second, edge)
        keep(field, j, image)
        prod[tile(3 * M + j), :] = total_of(a * b for a, b in zip(second, image))
        return carry

    for g in range(GROUPS):
        for copy in got_second[g]:
            copy.wait_recv()
        over_group(g, functools.partial(second_step, edges_of(1, g)), 0)
    for k in range(3 * M // 8, 4 * M // 8):
        fold(k)

    own = jnp.sum(jnp.transpose(flip[...]), axis=0, keepdims=True)
    for part, group in zip(parts, partners):
        members = len(group) + 1
        part[pl.ds(0, 1), :] = own
        copies = [
            send(part.at[pl.ds(0, 1)], part.at[pl.ds(n + 1, 1)], device)
            for n, device in enumerate(group)
        ]
        for copy in copies:
            copy.wait_recv()
        own = jnp.sum(part[pl.ds(0, members), :], axis=0, keepdims=True)

    zq = wide(own)
    zs = pltpu.roll(zq, C - M, 1)
    ds = pltpu.roll(zq, C - 2 * M, 1)
    dv = pltpu.roll(zq, C - 3 * M, 1)
    dq = zs - ds
    ratio = dq / zq
    second_part = (ds - dq * (zs / zq)) / (dv - ratio * dq)
    excess = (zs - dq * second_part) / zq

    def last_step(j, carry):
        turned = lax.rem(C - j, C)
        over = wide(pltpu.roll(excess, turned, 1)[:, :1])
        other = wide(pltpu.roll(second_part, turned, 1)[:, :1])
        main = 1.0 + over
        for c in range(D):
            at = tile(j * D + c)
            image = q0[at, :]
            x_ref[at, :] = main * z0[at, :] + other * d0[at, :]
            r_ref[at, :] = ((r0[at, :] - image) - over * image) - other * field[at, :]
        return carry

    for g in range(GROUPS):
        over_group(g, last_step, 0)
    for copy in sent:
        copy.wait_send()


def body(n_slab, n_sub, mode_shapes, span_stiff, chord_stiff, span_geo, chord_geo, ground, chord_len):
    stages = digit_stages(n_slab, n_sub)
    f32 = jnp.float32
    members = []
    for digits in stages:
        total = 1
        for _, _, size in digits:
            total *= size
        members.append(total)
    n_sends = 4 + 2 * (M // 8) + 8 * GROUPS + sum(members) - len(members)

    def big():
        return pltpu.VMEM((M * D * R, C), f32)

    rows = M * D
    scratch = [
        pltpu.SMEM(chord_len.shape, jnp.int32),
        pltpu.VMEM((M, D, R, C), jnp.bfloat16),
        pltpu.VMEM((D, R, C), f32),
        pltpu.VMEM((D, R, C), f32),
        pltpu.VMEM((R, C), f32),
        pltpu.VMEM((R, C), f32),
        pltpu.VMEM((D, R, C), f32),
        big(),
        big(),
        big(),
        big(),
        big(),
        pltpu.VMEM((D, R, C), f32),
        pltpu.VMEM((D, R, C), f32),
        pltpu.VMEM((21, R, C), f32),
        pltpu.VMEM((M * R, C), f32),
        pltpu.VMEM((M * R, C), f32),
        pltpu.VMEM((M * R, C), f32),
        pltpu.VMEM((M * R, C), f32),
        pltpu.VMEM((4 * M * R, C), f32),
        pltpu.VMEM((4 * M, C), f32),
        pltpu.VMEM((2, R, C), f32),
        pltpu.VMEM((R, C), f32),
        pltpu.VMEM((R, C), f32),
        pltpu.VMEM((rows, C), f32),
        pltpu.VMEM((rows, C), f32),
        pltpu.VMEM((rows, C), f32),
        pltpu.VMEM((rows, C), f32),
        pltpu.VMEM((3 * R, C), f32),
        pltpu.VMEM((3 * R, C), f32),
        pltpu.VMEM((3 * R, C), f32),
        pltpu.VMEM((M, C), f32),
        pltpu.VMEM((M, C), f32),
        pltpu.VMEM((R, C), f32),
        pltpu.VMEM((2 * M, C), f32),
        pltpu.VMEM((2 * M, C), f32),
        pltpu.VMEM((2 * M, C), f32),
        pltpu.VMEM((2 * M, C), f32),
        pltpu.VMEM((2, GROUPS, R, C), f32),
        pltpu.VMEM((2, GROUPS, R, C), f32),
        pltpu.VMEM((2, GROUPS, R, C), f32),
    ]
    scratch += [pltpu.VMEM((max(8, n), C), f32) for n in members]
    scratch += [
        pltpu.SemaphoreType.DMA((7,)),
        pltpu.SemaphoreType.DMA((n_sends,)),
        pltpu.SemaphoreType.DMA((n_sends,)),
    ]
    in_hbm = pl.BlockSpec(memory_space=pltpu.HBM)
    shape = jax.ShapeDtypeStruct((M * D * R, C), f32)
    adjoint, residual = pl.pallas_call(
        functools.partial(kernel, n_slab, n_sub, stages),
        out_shape=(shape, shape),
        in_specs=[in_hbm] * 7,
        out_specs=(pl.BlockSpec(memory_space=pltpu.VMEM),) * 2,
        scratch_shapes=scratch,
        compiler_params=pltpu.CompilerParams(
            collective_id=0, has_side_effects=True, vmem_limit_bytes=24 << 20
        ),
    )(mode_shapes, span_stiff, chord_stiff, span_geo, chord_geo, ground, chord_len)
    full = (M, D, R, C)
    return adjoint.reshape(full), residual.reshape(full)


def solution(mesh):
    sizes = (mesh.shape["slab"], mesh.shape["sub"])
    return jax.shard_map(
        functools.partial(body, *sizes),
        mesh=mesh,
        in_specs=(
            P(None, None, "slab", "sub"),
            P(None, "slab", "sub"),
            P(None, "slab", "sub"),
            P("slab", "sub"),
            P("slab", "sub"),
            P(None, "slab", "sub"),
            P(),
        ),
        out_specs=(P(None, None, "slab", "sub"), P(None, None, "slab", "sub")),
        check_vma=False,
    )
```

```python
import functools

import jax
import jax.numpy as jnp
from jax import lax
from jax.experimental import pallas as pl
from jax.experimental.pallas import tpu as pltpu
from jax.sharding import PartitionSpec as P

MESH = pl.DeviceIdType.MESH
D = 6
R, C = 8, 128
M = 32
GROUPS = 4
GM = M // GROUPS
UNROLL = 4


def digit_stages(n_slab, n_sub):
    core = 2
    z = 16 if n_slab % 32 == 0 else 1
    y = n_slab // (core * z)
    near = [("slab", 1, core), ("sub", 1, n_sub)]
    if y > 1:
        near.append(("slab", core * z, y))
    return [near, [("slab", core, z)]] if z > 1 else [near]


def stage_partners(digits, slab, sub):
    total = 1
    for _, _, size in digits:
        total *= size
    partners = []
    for offset in range(1, total):
        rest, at = offset, {"slab": slab, "sub": sub}
        for axis, stride, size in digits:
            step, rest = rest % size, rest // size
            digit = (at[axis] // stride) % size
            at[axis] = at[axis] + ((digit + step) % size - digit) * stride
        partners.append((at["slab"], at["sub"]))
    return partners


def total_of(terms):
    terms = list(terms)
    while len(terms) > 1:
        terms = [sum(terms[i : i + 2][1:], terms[i]) for i in range(0, len(terms), 2)]
    return terms[0]


def place(i, j):
    i, j = min(i, j), max(i, j)
    return i * D - i * (i - 1) // 2 + j - i


def kernel(
    n_slab,
    n_sub,
    stages,
    m_any,
    ss_any,
    cs_any,
    sg_any,
    cg_any,
    gr_any,
    len_any,
    x_ref,
    r_ref,
    len_ref,
    m_in,
    ss,
    cs,
    sg,
    cg,
    gr,
    field,
    r0,
    z0,
    q0,
    d0,
    ssb,
    csb,
    fac,
    ts,
    us,
    tc,
    uc,
    prod,
    flip,
    coef_send,
    coef_span,
    coef_chord,
    row_first,
    row_last,
    from_ahead,
    from_behind,
    col_own,
    col_ahead,
    col_behind,
    w_ahead,
    w_behind,
    w_col,
    t_send,
    u_send,
    u_ahead,
    t_behind,
    tu_send,
    tu_ahead,
    tu_behind,
    *rest,
):
    parts = rest[: len(stages)]
    in_sem, send_sem, recv_sem = rest[len(stages) :]
    slab, sub = lax.axis_index("slab"), lax.axis_index("sub")
    ahead = (lax.rem(slab + 1, n_slab), sub)
    behind = (lax.rem(slab + n_slab - 1, n_slab), sub)
    right = (slab, lax.rem(sub + 1, n_sub))
    left = (slab, lax.rem(sub + n_sub - 1, n_sub))
    partners = [stage_partners(digits, slab, sub) for digits in stages]

    loads = []
    for k, (source, target) in enumerate(
        ((m_any, m_in), (ss_any, ss), (cs_any, cs), (sg_any, sg), (cg_any, cg), (gr_any, gr), (len_any, len_ref))
    ):
        copy = pltpu.make_async_copy(source, target, in_sem.at[k])
        copy.start()
        loads.append(copy)

    barrier = pltpu.get_barrier_semaphore()
    greeted = [ahead, behind, right, left] + [p for group in partners for p in group]
    for device in greeted:
        pl.semaphore_signal(barrier, inc=1, device_id=device, device_id_type=MESH)

    row = lax.broadcasted_iota(jnp.int32, (R, C), 0)
    lane = lax.broadcasted_iota(jnp.int32, (R, C), 1)
    pair = lax.shift_right_logical(lane, 1)
    even = lane - 2 * pair == 0

    def tile(k):
        return pl.ds(pl.multiple_of(k * R, R), R)

    def wide(value):
        return jnp.broadcast_to(value, (R, C))

    def of_mode(ref, j):
        return [ref[tile(j * D + c), :] for c in range(D)]

    def keep(ref, j, vector):
        for c in range(D):
            ref[tile(j * D + c), :] = vector[c]

    def over_group(g, step, carry):
        def some(i, carry):
            for u in range(UNROLL):
                carry = step(g * GM + i * UNROLL + u, carry)
            return carry

        return lax.fori_loop(0, GM // UNROLL, some, carry)

    sent = []
    count = [0]

    def send(source, target, device):
        k = count[0]
        count[0] += 1
        copy = pltpu.make_async_remote_copy(
            src_ref=source,
            dst_ref=target,
            send_sem=send_sem.at[k],
            recv_sem=recv_sem.at[k],
            device_id=device,
            device_id_type=MESH,
        )
        copy.start()
        sent.append(copy)
        return copy

    loads[0].wait()

    def pack(i, packs):
        packs = list(packs)
        for u in range(UNROLL):
            j = i * UNROLL + u
            for c in range(D):
                value = m_in[j, c].astype(jnp.float32)
                field[tile(j * D + c), :] = value
                half = 32 * (c % 2)
                turned = pltpu.roll(value, 2 * (j + half) + 1, 1)
                packs[c // 2] = jnp.where(pair == j + half, turned, packs[c // 2])
        return tuple(packs)

    zero = jnp.zeros((R, C), jnp.float32)
    packs = lax.fori_loop(0, M // UNROLL, pack, (zero,) * 3)
    for v in range(3):
        col_own[pl.ds(v * R, R), :] = packs[v]
    for g in range(M // 8):
        for c in range(D):
            at = pl.ds((g * D + c) * 8, 8)
            row_first[at, :] = field[pl.ds((g * 8 * D + c) * R, 8, stride=D * R), :]
            row_last[at, :] = field[pl.ds((g * 8 * D + c) * R + R - 1, 8, stride=D * R), :]

    for copy in loads[1:]:
        copy.wait()
    span_coef, chord_coef = zero, zero
    for c in range(D + 1):
        mine = ss[c] if c < D else sg[...]
        span_coef = jnp.where(row == c, wide(mine[R - 1 :, :]), span_coef)
        mine = cs[c] if c < D else cg[...]
        chord_coef = jnp.where(lane == c, wide(mine[:, C - 1 :]), chord_coef)
    coef_send[0] = span_coef
    coef_send[1] = chord_coef

    pl.semaphore_wait(barrier, len(greeted))
    got_coef = [
        send(coef_send.at[0], coef_span, ahead),
        send(coef_send.at[1], coef_chord, right),
    ]
    got_cols = [send(col_own, col_behind, right), send(col_own, col_ahead, left)]
    got_rows = []
    for g in range(M // 8):
        at = pl.ds(g * 8 * D, 8 * D)
        got_rows.append(
            [
                send(row_last.at[at], from_behind.at[at], ahead),
                send(row_first.at[at], from_ahead.at[at], behind),
            ]
        )

    n_stations = n_slab * R
    first = slab * R
    length = jnp.zeros((R, C), jnp.int32)
    length_next = jnp.zeros((R, C), jnp.int32)
    length_prev = jnp.zeros((R, C), jnp.int32)
    for k in range(-1, R + 1):
        here = len_ref[jnp.clip(first + k, 0, n_stations - 1)]
        if 0 <= k < R:
            length = jnp.where(row == k, here, length)
        if k >= 1:
            length_next = jnp.where(row == k - 1, here, length_next)
        if k < R - 1:
            length_prev = jnp.where(row == k + 1, here, length_prev)
    column = lane + sub * C
    station = row + first
    one = jnp.ones((R, C), jnp.float32)
    span_live = jnp.where(
        (column < length) & (column < length_next) & (station < n_stations - 1), one, zero
    )
    span_live_b = jnp.where(
        (column < length) & (column < length_prev) & (station > 0), one, zero
    )
    chord_live = jnp.where(column + 1 < length, one, zero)
    chord_live_b = jnp.where((column < length) & (column > 0), one, zero)
    span_geo = sg[...] * span_live
    chord_geo = cg[...] * chord_live

    sg[...] = span_geo
    cg[...] = chord_geo

    def weigh(j, carry):
        modes = of_mode(field, j)
        jumps = [pltpu.roll(value, R - 1, 0) - value for value in modes]
        ts[tile(j), :] = total_of(jump * jump for jump in jumps) * sg[...]
        jumps = [pltpu.roll(value, C - 1, 1) - value for value in modes]
        tc[tile(j), :] = total_of(jump * jump for jump in jumps) * cg[...]
        return carry

    for g in range(GROUPS):
        over_group(g, weigh, 0)

    for copy in got_coef:
        copy.wait_recv()
    chord_ghost = coef_chord[...]
    for c in range(D):
        mine = ss[c]
        back = jnp.where(row == 0, wide(coef_span[pl.ds(c, 1), :]), pltpu.roll(mine, 1, 0))
        ssb[c] = back * span_live_b
        ss[c] = mine * span_live
        mine = cs[c]
        back = jnp.where(lane == 0, wide(chord_ghost[:, c : c + 1]), pltpu.roll(mine, 1, 1))
        csb[c] = back * chord_live_b
        cs[c] = mine * chord_live
    a_s = [ss[c] for c in range(D)]
    a_c = [cs[c] for c in range(D)]
    b_s = [ssb[c] for c in range(D)]
    b_c = [csb[c] for c in range(D)]
    low = [[None] * D for _ in range(D)]
    raw = [[None] * D for _ in range(D)]
    inverse = []
    for j in range(D):
        for i in range(j, D):
            entry = (a_s[i] * a_s[j] + b_s[i] * b_s[j]) + (a_c[i] * a_c[j] + b_c[i] * b_c[j])
            if i == j:
                entry = entry + gr[i]
            for n in range(j):
                entry = entry - raw[i][n] * low[j][n]
            raw[i][j] = entry
        inverse.append(1.0 / raw[j][j])
        for i in range(j + 1, D):
            low[i][j] = raw[i][j] * inverse[j]
    unit = [[None] * D for _ in range(D)]
    for j in range(D):
        for i in range(j + 1, D):
            entry = low[i][j]
            for n in range(j + 1, i):
                entry = entry + low[i][n] * unit[n][j]
            unit[i][j] = -entry
    scaled = [[None] * D for _ in range(D)]
    for k in range(D):
        for i in range(k):
            scaled[k][i] = unit[k][i] * inverse[k]
        scaled[k][k] = inverse[k]
    for i in range(D):
        for j in range(i, D):
            terms = [scaled[j][i] if i < j else inverse[j]]
            terms += [scaled[k][i] * unit[k][j] for k in range(j + 1, D)]
            fac[place(i, j)] = total_of(terms)

    def solve(vector):
        return [total_of(fac[place(i, j)] * vector[j] for j in range(D)) for i in range(D)]

    def dots(j, vector, packed):
        t_s = total_of(ss[c] * vector[c] for c in range(D))
        u_s = total_of(ssb[c] * vector[c] for c in range(D))
        t_c = total_of(cs[c] * vector[c] for c in range(D))
        u_c = total_of(csb[c] * vector[c] for c in range(D))
        ts[tile(j), :] = t_s
        us[tile(j), :] = u_s
        tc[tile(j), :] = t_c
        uc[tile(j), :] = u_c
        turned = pltpu.roll(jnp.where(lane == 0, u_c, t_c), 2 * j + 1, 1)
        return jnp.where(pair == j, turned, packed)

    def send_dots(turn, g, packed):
        at = pl.ds(turn * M + g * GM, GM)
        for b in range(GM // 8):
            from_mode = g * GM + b * 8
            to = pl.ds(turn * M + from_mode, 8)
            t_send[to, :] = ts[pl.ds(from_mode * R + R - 1, 8, stride=R), :]
            u_send[to, :] = us[pl.ds(from_mode * R, 8, stride=R), :]
        tu_send[turn, g] = packed
        return [
            send(t_send.at[at], t_behind.at[at], ahead),
            send(u_send.at[at], u_ahead.at[at], behind),
            send(tu_send.at[turn, g], tu_behind.at[turn, g], right),
            send(tu_send.at[turn, g], tu_ahead.at[turn, g], left),
        ]

    def edges_of(turn, g):
        return jnp.where(
            even,
            pltpu.roll(tu_ahead[turn, g], C - 1, 1),
            pltpu.roll(tu_behind[turn, g], 1, 1),
        )

    def operate(turn, j, vector, edge):
        t_s, u_s, t_c, u_c = ts[tile(j), :], us[tile(j), :], tc[tile(j), :], uc[tile(j), :]
        at = pl.ds(turn * M + j, 1)
        edge = pltpu.roll(edge, C - 1 - 2 * j, 1)
        u_s_next = jnp.where(row == R - 1, wide(u_ahead[at, :]), pltpu.roll(u_s, R - 1, 0))
        t_s_prev = jnp.where(row == 0, wide(t_behind[at, :]), pltpu.roll(t_s, 1, 0))
        u_c_next = jnp.where(lane == C - 1, edge, pltpu.roll(u_c, C - 1, 1))
        t_c_prev = jnp.where(lane == 0, edge, pltpu.roll(t_c, 1, 1))
        e_s, e_sb = u_s_next - t_s, u_s - t_s_prev
        e_c, e_cb = u_c_next - t_c, u_c - t_c_prev
        return [
            (gr[c] * vector[c] + (ssb[c] * e_sb - ss[c] * e_s)) + (csb[c] * e_cb - cs[c] * e_c)
            for c in range(D)
        ]

    for copy in got_cols:
        copy.wait_recv()
    square = None
    for v in range(3):
        at = pl.ds(v * R, R)
        across = jnp.where(
            even, pltpu.roll(col_ahead[at, :], C - 1, 1), pltpu.roll(col_behind[at, :], 1, 1)
        )
        jump = across - col_own[at, :]
        square = jump * jump if square is None else square + jump * jump
    square = square + pltpu.roll(square, C // 2, 1)
    geo_b = chord_ghost[:, D : D + 1] * chord_live_b[:, :1]
    w_col[...] = square * jnp.where(even, wide(chord_geo[:, C - 1 :]), wide(geo_b))
    geo_ahead = jnp.broadcast_to(span_geo[R - 1 :, :], (8, C))
    geo_behind = jnp.broadcast_to(coef_span[pl.ds(D, 1), :] * span_live_b[:1, :], (8, C))

    def load_step(j, packed):
        edge = pltpu.roll(w_col[...], C - 1 - 2 * j, 1)
        w_s = jnp.where(row == R - 1, wide(w_ahead[pl.ds(j, 1), :]), ts[tile(j), :])
        w_c = jnp.where(lane == C - 1, edge, tc[tile(j), :])
        w_sb = jnp.where(row == 0, wide(w_behind[pl.ds(j, 1), :]), pltpu.roll(w_s, 1, 0))
        w_cb = jnp.where(lane == 0, edge, pltpu.roll(w_c, 1, 1))
        load = [
            (ssb[c] * w_sb - ss[c] * w_s) + (csb[c] * w_cb - cs[c] * w_c) for c in range(D)
        ]
        first_z = solve(load)
        keep(r0, j, load)
        keep(z0, j, first_z)
        return dots(j, first_z, packed)

    got_first = []
    for g in range(GROUPS):
        for b in range(GM // 8):
            block = g * (GM // 8) + b
            for copy in got_rows[block]:
                copy.wait_recv()
            to_ahead, to_behind = [], []
            for c in range(D):
                at = pl.ds((block * D + c) * 8, 8)
                jump = from_ahead[at, :] - row_last[at, :]
                to_ahead.append(jump * jump)
                jump = row_first[at, :] - from_behind[at, :]
                to_behind.append(jump * jump)
            w_ahead[pl.ds(block * 8, 8), :] = total_of(to_ahead) * geo_ahead
            w_behind[pl.ds(block * 8, 8), :] = total_of(to_behind) * geo_behind
        got_first.append(send_dots(0, g, over_group(g, load_step, zero)))

    def first_step(edge, j, packed):
        z = of_mode(z0, j)
        image = operate(0, j, z, edge)
        left_over = [a - b for a, b in zip(of_mode(r0, j), image)]
        second = solve(left_over)
        keep(q0, j, image)
        keep(d0, j, second)
        prod[tile(j), :] = total_of(a * b for a, b in zip(z, image))
        prod[tile(M + j), :] = total_of(a * b for a, b in zip(z, left_over))
        prod[tile(2 * M + j), :] = total_of(a * b for a, b in zip(second, left_over))
        return dots(j, second, packed)

    got_second = []
    for g in range(GROUPS):
        for copy in got_first[g]:
            copy.wait_recv()
        edge = edges_of(0, g)
        packed = over_group(g, functools.partial(first_step, edge), zero)
        got_second.append(send_dots(1, g, packed))

    def fold(k):
        rows = [prod[pl.ds(k * 8 * R + n, 8, stride=R), :] for n in range(R)]
        flip[pl.ds(k * 8, 8), :] = total_of(rows)

    for k in range(3 * M // 8):
        fold(k)

    def second_step(edge, j, carry):
        second = of_mode(d0, j)
        image = operate(1, j, second, edge)
        keep(field, j, image)
        prod[tile(3 * M + j), :] = total_of(a * b for a, b in zip(second, image))
        return carry

    for g in range(GROUPS):
        for copy in got_second[g]:
            copy.wait_recv()
        over_group(g, functools.partial(second_step, edges_of(1, g)), 0)
    for k in range(3 * M // 8, 4 * M // 8):
        fold(k)

    own = jnp.sum(jnp.transpose(flip[...]), axis=0, keepdims=True)
    for part, group in zip(parts, partners):
        members = len(group) + 1
        part[pl.ds(0, 1), :] = own
        copies = [
            send(part.at[pl.ds(0, 1)], part.at[pl.ds(n + 1, 1)], device)
            for n, device in enumerate(group)
        ]
        for copy in copies:
            copy.wait_recv()
        own = jnp.sum(part[pl.ds(0, members), :], axis=0, keepdims=True)

    zq = wide(own)
    zs = pltpu.roll(zq, C - M, 1)
    ds = pltpu.roll(zq, C - 2 * M, 1)
    dv = pltpu.roll(zq, C - 3 * M, 1)
    dq = zs - ds
    ratio = dq / zq
    second_part = (ds - dq * (zs / zq)) / (dv - ratio * dq)
    excess = (zs - dq * second_part) / zq

    def last_step(j, carry):
        turned = lax.rem(C - j, C)
        over = wide(pltpu.roll(excess, turned, 1)[:, :1])
        other = wide(pltpu.roll(second_part, turned, 1)[:, :1])
        main = 1.0 + over
        for c in range(D):
            at = tile(j * D + c)
            image = q0[at, :]
            x_ref[at, :] = main * z0[at, :] + other * d0[at, :]
            r_ref[at, :] = ((r0[at, :] - image) - over * image) - other * field[at, :]
        return carry

    for g in range(GROUPS):
        over_group(g, last_step, 0)
    for copy in sent:
        copy.wait_send()


def body(n_slab, n_sub, mode_shapes, span_stiff, chord_stiff, span_geo, chord_geo, ground, chord_len):
    stages = digit_stages(n_slab, n_sub)
    f32 = jnp.float32
    members = []
    for digits in stages:
        total = 1
        for _, _, size in digits:
            total *= size
        members.append(total)
    n_sends = 4 + 2 * (M // 8) + 8 * GROUPS + sum(members) - len(members)

    def big():
        return pltpu.VMEM((M * D * R, C), f32)

    rows = M * D
    scratch = [
        pltpu.SMEM(chord_len.shape, jnp.int32),
        pltpu.VMEM((M, D, R, C), jnp.bfloat16),
        pltpu.VMEM((D, R, C), f32),
        pltpu.VMEM((D, R, C), f32),
        pltpu.VMEM((R, C), f32),
        pltpu.VMEM((R, C), f32),
        pltpu.VMEM((D, R, C), f32),
        big(),
        big(),
        big(),
        big(),
        big(),
        pltpu.VMEM((D, R, C), f32),
        pltpu.VMEM((D, R, C), f32),
        pltpu.VMEM((21, R, C), f32),
        pltpu.VMEM((M * R, C), f32),
        pltpu.VMEM((M * R, C), f32),
        pltpu.VMEM((M * R, C), f32),
        pltpu.VMEM((M * R, C), f32),
        pltpu.VMEM((4 * M * R, C), f32),
        pltpu.VMEM((4 * M, C), f32),
        pltpu.VMEM((2, R, C), f32),
        pltpu.VMEM((R, C), f32),
        pltpu.VMEM((R, C), f32),
        pltpu.VMEM((rows, C), f32),
        pltpu.VMEM((rows, C), f32),
        pltpu.VMEM((rows, C), f32),
        pltpu.VMEM((rows, C), f32),
        pltpu.VMEM((3 * R, C), f32),
        pltpu.VMEM((3 * R, C), f32),
        pltpu.VMEM((3 * R, C), f32),
        pltpu.VMEM((M, C), f32),
        pltpu.VMEM((M, C), f32),
        pltpu.VMEM((R, C), f32),
        pltpu.VMEM((2 * M, C), f32),
        pltpu.VMEM((2 * M, C), f32),
        pltpu.VMEM((2 * M, C), f32),
        pltpu.VMEM((2 * M, C), f32),
        pltpu.VMEM((2, GROUPS, R, C), f32),
        pltpu.VMEM((2, GROUPS, R, C), f32),
        pltpu.VMEM((2, GROUPS, R, C), f32),
    ]
    scratch += [pltpu.VMEM((max(8, n), C), f32) for n in members]
    scratch += [
        pltpu.SemaphoreType.DMA((7,)),
        pltpu.SemaphoreType.DMA((n_sends,)),
        pltpu.SemaphoreType.DMA((n_sends,)),
    ]
    operands = [
        pltpu.with_memory_space_constraint(value, pltpu.HBM)
        for value in (
            mode_shapes, span_stiff, chord_stiff, span_geo, chord_geo, ground, chord_len
        )
    ]
    in_hbm = pl.BlockSpec(memory_space=pltpu.HBM)
    shape = jax.ShapeDtypeStruct((M * D * R, C), f32)
    adjoint, residual = pl.pallas_call(
        functools.partial(kernel, n_slab, n_sub, stages),
        out_shape=(shape, shape),
        in_specs=[in_hbm] * 7,
        out_specs=(pl.BlockSpec(memory_space=pltpu.VMEM),) * 2,
        scratch_shapes=scratch,
        compiler_params=pltpu.CompilerParams(
            collective_id=0, has_side_effects=True, vmem_limit_bytes=24 << 20
        ),
    )(*operands)
    full = (M, D, R, C)
    return adjoint.reshape(full), residual.reshape(full)


def solution(mesh):
    sizes = (mesh.shape["slab"], mesh.shape["sub"])
    return jax.shard_map(
        functools.partial(body, *sizes),
        mesh=mesh,
        in_specs=(
            P(None, None, "slab", "sub"),
            P(None, "slab", "sub"),
            P(None, "slab", "sub"),
            P("slab", "sub"),
            P("slab", "sub"),
            P(None, "slab", "sub"),
            P(),
        ),
        out_specs=(P(None, None, "slab", "sub"), P(None, None, "slab", "sub")),
        check_vma=False,
    )
```

```python
import functools

import jax
import jax.numpy as jnp
from jax import lax
from jax.experimental import pallas as pl
from jax.experimental.pallas import tpu as pltpu
from jax.sharding import PartitionSpec as P

MESH = pl.DeviceIdType.MESH
D = 6
R, C = 8, 128
M = 32
GROUPS = 4
GM = M // GROUPS
UNROLL = 8


def digits_of(n_slab):
    core = 2
    z = 16 if n_slab % 32 == 0 else 4 if n_slab % 8 == 0 else 1
    return core, z, n_slab // (core * z)


def digit_stages(n_slab, n_sub):
    core, z, y = digits_of(n_slab)
    return [[("slab", 1, core), ("sub", 1, n_sub), ("slab", core * z, y)], [("slab", core, z)]]


def stage_partners(digits, slab, sub):
    total = 1
    for _, _, size in digits:
        total *= size
    partners = []
    for offset in range(1, total):
        rest, at = offset, {"slab": slab, "sub": sub}
        for axis, stride, size in digits:
            step, rest = rest % size, rest // size
            digit = (at[axis] // stride) % size
            at[axis] = at[axis] + ((digit + step) % size - digit) * stride
        partners.append((at["slab"], at["sub"]))
    return partners


def total_of(terms):
    terms = list(terms)
    while len(terms) > 1:
        terms = [sum(terms[i : i + 2][1:], terms[i]) for i in range(0, len(terms), 2)]
    return terms[0]


def place(i, j):
    i, j = min(i, j), max(i, j)
    return i * D - i * (i - 1) // 2 + j - i


def kernel(
    n_slab,
    n_sub,
    stages,
    m_any,
    ss_any,
    cs_any,
    sg_any,
    cg_any,
    gr_any,
    len_any,
    r0,
    z0,
    q0,
    d0,
    image2,
    over,
    other,
    len_ref,
    m_in,
    ss,
    cs,
    sg,
    cg,
    gr,
    field,
    ssb,
    csb,
    fac,
    ts,
    us,
    tc,
    uc,
    prod,
    flip,
    coef_send,
    coef_span,
    coef_chord,
    row_first,
    row_last,
    from_ahead,
    from_behind,
    col_own,
    col_ahead,
    col_behind,
    w_ahead,
    w_behind,
    w_col,
    t_send,
    u_send,
    u_ahead,
    t_behind,
    tu_send,
    tu_ahead,
    tu_behind,
    *rest,
):
    parts = rest[: len(stages)]
    in_sem, send_sem, recv_sem, here_sem = rest[len(stages) :]
    slab, sub = lax.axis_index("slab"), lax.axis_index("sub")
    ahead = (lax.rem(slab + 1, n_slab), sub)
    behind = (lax.rem(slab + n_slab - 1, n_slab), sub)
    right = (slab, lax.rem(sub + 1, n_sub))
    left = (slab, lax.rem(sub + n_sub - 1, n_sub))
    partners = [stage_partners(digits, slab, sub) for digits in stages]

    loads = []
    for k, (source, target) in enumerate(
        ((m_any, m_in), (ss_any, ss), (cs_any, cs), (sg_any, sg), (cg_any, cg), (gr_any, gr), (len_any, len_ref))
    ):
        copy = pltpu.make_async_copy(source, target, in_sem.at[k])
        copy.start()
        loads.append(copy)

    core, z_size, y_size = digits_of(n_slab)
    flat = stage_partners([("slab", 1, core), ("sub", 1, n_sub)], slab, sub)
    ring_y = stage_partners([("slab", core * z_size, y_size)], slab, sub)
    ring_z = stage_partners([("slab", core, z_size)], slab, sub)

    def along_z(distance):
        return [ring_z[distance - 1], ring_z[z_size - distance - 1]] if z_size > 1 else []

    def tell(semaphore, devices):
        for device in devices:
            pl.semaphore_signal(semaphore, inc=1, device_id=device, device_id_type=MESH)

    barrier = pltpu.get_barrier_semaphore()
    greeted = [ahead, behind] + flat + ring_y + along_z(1)
    tell(barrier, greeted)

    reaches = [distance for distance in (1, 2, 4) if 2 * distance < z_size]
    told = [0]

    def widen():
        if 0 < told[0] <= len(reaches):
            pl.semaphore_wait(here_sem.at[told[0]], 2)
        if told[0] < len(reaches):
            tell(here_sem.at[told[0] + 1], along_z(reaches[told[0]]))
        told[0] += 1

    row = lax.broadcasted_iota(jnp.int32, (R, C), 0)
    lane = lax.broadcasted_iota(jnp.int32, (R, C), 1)
    pair = lax.shift_right_logical(lane, 1)
    even = lane - 2 * pair == 0

    def tile(k):
        return pl.ds(pl.multiple_of(k * R, R), R)

    def wide(value):
        return jnp.broadcast_to(value, (R, C))

    def of_mode(ref, j):
        return [ref[tile(j * D + c), :] for c in range(D)]

    def keep(ref, j, vector):
        for c in range(D):
            ref[tile(j * D + c), :] = vector[c]

    def over_group(g, step, carry):
        def some(i, carry):
            for u in range(UNROLL):
                carry = step(g * GM + i * UNROLL + u, carry)
            return carry

        return lax.fori_loop(0, GM // UNROLL, some, carry)

    sent = []
    count = [0]

    def send(source, target, device):
        k = count[0]
        count[0] += 1
        copy = pltpu.make_async_remote_copy(
            src_ref=source,
            dst_ref=target,
            send_sem=send_sem.at[k],
            recv_sem=recv_sem.at[k],
            device_id=device,
            device_id_type=MESH,
        )
        copy.start()
        sent.append(copy)
        return copy

    loads[0].wait()

    def pack(i, packs):
        packs = list(packs)
        for u in range(UNROLL):
            j = i * UNROLL + u
            for c in range(D):
                value = m_in[j, c].astype(jnp.float32)
                field[tile(j * D + c), :] = value
                half = 32 * (c % 2)
                turned = pltpu.roll(value, 2 * (j + half) + 1, 1)
                packs[c // 2] = jnp.where(pair == j + half, turned, packs[c // 2])
        return tuple(packs)

    zero = jnp.zeros((R, C), jnp.float32)
    packs = lax.fori_loop(0, M // UNROLL, pack, (zero,) * 3)
    for v in range(3):
        col_own[pl.ds(v * R, R), :] = packs[v]
    for g in range(M // 8):
        for c in range(D):
            at = pl.ds((g * D + c) * 8, 8)
            row_first[at, :] = field[pl.ds((g * 8 * D + c) * R, 8, stride=D * R), :]
            row_last[at, :] = field[pl.ds((g * 8 * D + c) * R + R - 1, 8, stride=D * R), :]

    for copy in loads[1:]:
        copy.wait()
    span_coef, chord_coef = zero, zero
    for c in range(D + 1):
        mine = ss[c] if c < D else sg[...]
        span_coef = jnp.where(row == c, wide(mine[R - 1 :, :]), span_coef)
        mine = cs[c] if c < D else cg[...]
        chord_coef = jnp.where(lane == c, wide(mine[:, C - 1 :]), chord_coef)
    coef_send[0] = span_coef
    coef_send[1] = chord_coef

    pl.semaphore_wait(barrier, len(greeted))
    tell(here_sem.at[0], flat)
    widen()
    got_coef = [
        send(coef_send.at[0], coef_span, ahead),
        send(coef_send.at[1], coef_chord, right),
    ]
    got_cols = [send(col_own, col_behind, right), send(col_own, col_ahead, left)]
    got_rows = []
    for g in range(M // 8):
        at = pl.ds(g * 8 * D, 8 * D)
        got_rows.append(
            [
                send(row_last.at[at], from_behind.at[at], ahead),
                send(row_first.at[at], from_ahead.at[at], behind),
            ]
        )

    n_stations = n_slab * R
    first = slab * R
    length = jnp.zeros((R, C), jnp.int32)
    length_next = jnp.zeros((R, C), jnp.int32)
    length_prev = jnp.zeros((R, C), jnp.int32)
    for k in range(-1, R + 1):
        here = len_ref[jnp.clip(first + k, 0, n_stations - 1)]
        if 0 <= k < R:
            length = jnp.where(row == k, here, length)
        if k >= 1:
            length_next = jnp.where(row == k - 1, here, length_next)
        if k < R - 1:
            length_prev = jnp.where(row == k + 1, here, length_prev)
    column = lane + sub * C
    station = row + first
    one = jnp.ones((R, C), jnp.float32)
    span_live = jnp.where(
        (column < length) & (column < length_next) & (station < n_stations - 1), one, zero
    )
    span_live_b = jnp.where(
        (column < length) & (column < length_prev) & (station > 0), one, zero
    )
    chord_live = jnp.where(column + 1 < length, one, zero)
    chord_live_b = jnp.where((column < length) & (column > 0), one, zero)
    span_geo = sg[...] * span_live
    chord_geo = cg[...] * chord_live

    sg[...] = span_geo
    cg[...] = chord_geo

    def weigh(j, carry):
        modes = of_mode(field, j)
        jumps = [pltpu.roll(value, R - 1, 0) - value for value in modes]
        ts[tile(j), :] = total_of(jump * jump for jump in jumps) * sg[...]
        jumps = [pltpu.roll(value, C - 1, 1) - value for value in modes]
        tc[tile(j), :] = total_of(jump * jump for jump in jumps) * cg[...]
        return carry

    for g in range(GROUPS):
        over_group(g, weigh, 0)

    for copy in got_coef:
        copy.wait_recv()
    widen()
    chord_ghost = coef_chord[...]
    for c in range(D):
        mine = ss[c]
        back = jnp.where(row == 0, wide(coef_span[pl.ds(c, 1), :]), pltpu.roll(mine, 1, 0))
        ssb[c] = back * span_live_b
        ss[c] = mine * span_live
        mine = cs[c]
        back = jnp.where(lane == 0, wide(chord_ghost[:, c : c + 1]), pltpu.roll(mine, 1, 1))
        csb[c] = back * chord_live_b
        cs[c] = mine * chord_live
    a_s = [ss[c] for c in range(D)]
    a_c = [cs[c] for c in range(D)]
    b_s = [ssb[c] for c in range(D)]
    b_c = [csb[c] for c in range(D)]
    low = [[None] * D for _ in range(D)]
    raw = [[None] * D for _ in range(D)]
    inverse = []
    for j in range(D):
        for i in range(j, D):
            entry = (a_s[i] * a_s[j] + b_s[i] * b_s[j]) + (a_c[i] * a_c[j] + b_c[i] * b_c[j])
            if i == j:
                entry = entry + gr[i]
            for n in range(j):
                entry = entry - raw[i][n] * low[j][n]
            raw[i][j] = entry
        inverse.append(1.0 / raw[j][j])
        for i in range(j + 1, D):
            low[i][j] = raw[i][j] * inverse[j]
    unit = [[None] * D for _ in range(D)]
    for j in range(D):
        for i in range(j + 1, D):
            entry = low[i][j]
            for n in range(j + 1, i):
                entry = entry + low[i][n] * unit[n][j]
            unit[i][j] = -entry
    scaled = [[None] * D for _ in range(D)]
    for k in range(D):
        for i in range(k):
            scaled[k][i] = unit[k][i] * inverse[k]
        scaled[k][k] = inverse[k]
    for i in range(D):
        for j in range(i, D):
            terms = [scaled[j][i] if i < j else inverse[j]]
            terms += [scaled[k][i] * unit[k][j] for k in range(j + 1, D)]
            fac[place(i, j)] = total_of(terms)

    def solve(vector):
        return [total_of(fac[place(i, j)] * vector[j] for j in range(D)) for i in range(D)]

    def dots(j, vector, packed):
        t_s = total_of(ss[c] * vector[c] for c in range(D))
        u_s = total_of(ssb[c] * vector[c] for c in range(D))
        t_c = total_of(cs[c] * vector[c] for c in range(D))
        u_c = total_of(csb[c] * vector[c] for c in range(D))
        ts[tile(j), :] = t_s
        us[tile(j), :] = u_s
        tc[tile(j), :] = t_c
        uc[tile(j), :] = u_c
        turned = pltpu.roll(jnp.where(lane == 0, u_c, t_c), 2 * j + 1, 1)
        return jnp.where(pair == j, turned, packed)

    def send_dots(turn, g, packed):
        at = pl.ds(turn * M + g * GM, GM)
        for b in range(GM // 8):
            from_mode = g * GM + b * 8
            to = pl.ds(turn * M + from_mode, 8)
            t_send[to, :] = ts[pl.ds(from_mode * R + R - 1, 8, stride=R), :]
            u_send[to, :] = us[pl.ds(from_mode * R, 8, stride=R), :]
        tu_send[turn, g] = packed
        return [
            send(t_send.at[at], t_behind.at[at], ahead),
            send(u_send.at[at], u_ahead.at[at], behind),
            send(tu_send.at[turn, g], tu_behind.at[turn, g], right),
            send(tu_send.at[turn, g], tu_ahead.at[turn, g], left),
        ]

    def edges_of(turn, g):
        return jnp.where(
            even,
            pltpu.roll(tu_ahead[turn, g], C - 1, 1),
            pltpu.roll(tu_behind[turn, g], 1, 1),
        )

    def operate(turn, j, vector, edge):
        t_s, u_s, t_c, u_c = ts[tile(j), :], us[tile(j), :], tc[tile(j), :], uc[tile(j), :]
        at = pl.ds(turn * M + j, 1)
        edge = pltpu.roll(edge, C - 1 - 2 * j, 1)
        u_s_next = jnp.where(row == R - 1, wide(u_ahead[at, :]), pltpu.roll(u_s, R - 1, 0))
        t_s_prev = jnp.where(row == 0, wide(t_behind[at, :]), pltpu.roll(t_s, 1, 0))
        u_c_next = jnp.where(lane == C - 1, edge, pltpu.roll(u_c, C - 1, 1))
        t_c_prev = jnp.where(lane == 0, edge, pltpu.roll(t_c, 1, 1))
        e_s, e_sb = u_s_next - t_s, u_s - t_s_prev
        e_c, e_cb = u_c_next - t_c, u_c - t_c_prev
        return [
            (gr[c] * vector[c] + (ssb[c] * e_sb - ss[c] * e_s)) + (csb[c] * e_cb - cs[c] * e_c)
            for c in range(D)
        ]

    for copy in got_cols:
        copy.wait_recv()
    square = None
    for v in range(3):
        at = pl.ds(v * R, R)
        across = jnp.where(
            even, pltpu.roll(col_ahead[at, :], C - 1, 1), pltpu.roll(col_behind[at, :], 1, 1)
        )
        jump = across - col_own[at, :]
        square = jump * jump if square is None else square + jump * jump
    square = square + pltpu.roll(square, C // 2, 1)
    geo_b = chord_ghost[:, D : D + 1] * chord_live_b[:, :1]
    w_col[...] = square * jnp.where(even, wide(chord_geo[:, C - 1 :]), wide(geo_b))
    geo_ahead = jnp.broadcast_to(span_geo[R - 1 :, :], (8, C))
    geo_behind = jnp.broadcast_to(coef_span[pl.ds(D, 1), :] * span_live_b[:1, :], (8, C))

    def load_step(j, packed):
        edge = pltpu.roll(w_col[...], C - 1 - 2 * j, 1)
        w_s = jnp.where(row == R - 1, wide(w_ahead[pl.ds(j, 1), :]), ts[tile(j), :])
        w_c = jnp.where(lane == C - 1, edge, tc[tile(j), :])
        w_sb = jnp.where(row == 0, wide(w_behind[pl.ds(j, 1), :]), pltpu.roll(w_s, 1, 0))
        w_cb = jnp.where(lane == 0, edge, pltpu.roll(w_c, 1, 1))
        load = [
            (ssb[c] * w_sb - ss[c] * w_s) + (csb[c] * w_cb - cs[c] * w_c) for c in range(D)
        ]
        first_z = solve(load)
        keep(r0, j, load)
        keep(z0, j, first_z)
        return dots(j, first_z, packed)

    got_first = []
    for g in range(GROUPS):
        for b in range(GM // 8):
            block = g * (GM // 8) + b
            for copy in got_rows[block]:
                copy.wait_recv()
            to_ahead, to_behind = [], []
            for c in range(D):
                at = pl.ds((block * D + c) * 8, 8)
                jump = from_ahead[at, :] - row_last[at, :]
                to_ahead.append(jump * jump)
                jump = row_first[at, :] - from_behind[at, :]
                to_behind.append(jump * jump)
            w_ahead[pl.ds(block * 8, 8), :] = total_of(to_ahead) * geo_ahead
            w_behind[pl.ds(block * 8, 8), :] = total_of(to_behind) * geo_behind
        got_first.append(send_dots(0, g, over_group(g, load_step, zero)))

    def first_step(edge, j, packed):
        z = of_mode(z0, j)
        image = operate(0, j, z, edge)
        left_over = [a - b for a, b in zip(of_mode(r0, j), image)]
        second = solve(left_over)
        keep(q0, j, image)
        keep(d0, j, second)
        prod[tile(j), :] = total_of(a * b for a, b in zip(z, image))
        prod[tile(M + j), :] = total_of(a * b for a, b in zip(z, left_over))
        prod[tile(2 * M + j), :] = total_of(a * b for a, b in zip(second, left_over))
        return dots(j, second, packed)

    widen()
    got_second = []
    for g in range(GROUPS):
        for copy in got_first[g]:
            copy.wait_recv()
        edge = edges_of(0, g)
        packed = over_group(g, functools.partial(first_step, edge), zero)
        got_second.append(send_dots(1, g, packed))

    def fold(k):
        rows = [prod[pl.ds(k * 8 * R + n, 8, stride=R), :] for n in range(R)]
        flip[pl.ds(k * 8, 8), :] = total_of(rows)

    for k in range(3 * M // 8):
        fold(k)

    def second_step(edge, j, carry):
        second = of_mode(d0, j)
        image = operate(1, j, second, edge)
        keep(image2, j, image)
        prod[tile(3 * M + j), :] = total_of(a * b for a, b in zip(second, image))
        return carry

    for g in range(GROUPS):
        for copy in got_second[g]:
            copy.wait_recv()
        over_group(g, functools.partial(second_step, edges_of(1, g)), 0)
    for k in range(3 * M // 8, 4 * M // 8):
        fold(k)

    pl.semaphore_wait(here_sem.at[0], len(flat))
    while told[0] <= len(reaches):
        widen()
    own = jnp.sum(jnp.transpose(flip[...]), axis=0, keepdims=True)
    for part, group in zip(parts, partners):
        members = len(group) + 1
        part[pl.ds(0, 1), :] = own
        copies = [
            send(part.at[pl.ds(0, 1)], part.at[pl.ds(n + 1, 1)], device)
            for n, device in enumerate(group)
        ]
        for copy in copies:
            copy.wait_recv()
        own = jnp.sum(part[pl.ds(0, members), :], axis=0, keepdims=True)

    zq = wide(own)
    zs = pltpu.roll(zq, C - M, 1)
    ds = pltpu.roll(zq, C - 2 * M, 1)
    dv = pltpu.roll(zq, C - 3 * M, 1)
    dq = zs - ds
    ratio = dq / zq
    second_part = (ds - dq * (zs / zq)) / (dv - ratio * dq)
    excess = (zs - dq * second_part) / zq

    def spread(j, carry):
        over[tile(j), :] = wide(pltpu.roll(excess, C - 1 - j, 1)[:, C - 1 :])
        other[tile(j), :] = wide(pltpu.roll(second_part, C - 1 - j, 1)[:, C - 1 :])
        return carry

    for g in range(GROUPS):
        over_group(g, spread, 0)
    for copy in sent:
        copy.wait_send()


def body(n_slab, n_sub, mode_shapes, span_stiff, chord_stiff, span_geo, chord_geo, ground, chord_len):
    stages = digit_stages(n_slab, n_sub)
    f32 = jnp.float32
    members = []
    for digits in stages:
        total = 1
        for _, _, size in digits:
            total *= size
        members.append(total)
    n_sends = 4 + 2 * (M // 8) + 8 * GROUPS + sum(members) - len(members)

    def big():
        return pltpu.VMEM((M * D * R, C), f32)

    rows = M * D
    scratch = [
        pltpu.SMEM(chord_len.shape, jnp.int32),
        pltpu.VMEM((M, D, R, C), jnp.bfloat16),
        pltpu.VMEM((D, R, C), f32),
        pltpu.VMEM((D, R, C), f32),
        pltpu.VMEM((R, C), f32),
        pltpu.VMEM((R, C), f32),
        pltpu.VMEM((D, R, C), f32),
        big(),
        pltpu.VMEM((D, R, C), f32),
        pltpu.VMEM((D, R, C), f32),
        pltpu.VMEM((21, R, C), f32),
        pltpu.VMEM((M * R, C), f32),
        pltpu.VMEM((M * R, C), f32),
        pltpu.VMEM((M * R, C), f32),
        pltpu.VMEM((M * R, C), f32),
        pltpu.VMEM((4 * M * R, C), f32),
        pltpu.VMEM((4 * M, C), f32),
        pltpu.VMEM((2, R, C), f32),
        pltpu.VMEM((R, C), f32),
        pltpu.VMEM((R, C), f32),
        pltpu.VMEM((rows, C), f32),
        pltpu.VMEM((rows, C), f32),
        pltpu.VMEM((rows, C), f32),
        pltpu.VMEM((rows, C), f32),
        pltpu.VMEM((3 * R, C), f32),
        pltpu.VMEM((3 * R, C), f32),
        pltpu.VMEM((3 * R, C), f32),
        pltpu.VMEM((M, C), f32),
        pltpu.VMEM((M, C), f32),
        pltpu.VMEM((R, C), f32),
        pltpu.VMEM((2 * M, C), f32),
        pltpu.VMEM((2 * M, C), f32),
        pltpu.VMEM((2 * M, C), f32),
        pltpu.VMEM((2 * M, C), f32),
        pltpu.VMEM((2, GROUPS, R, C), f32),
        pltpu.VMEM((2, GROUPS, R, C), f32),
        pltpu.VMEM((2, GROUPS, R, C), f32),
    ]
    scratch += [pltpu.VMEM((max(8, n), C), f32) for n in members]
    scratch += [
        pltpu.SemaphoreType.DMA((7,)),
        pltpu.SemaphoreType.DMA((n_sends,)),
        pltpu.SemaphoreType.DMA((n_sends,)),
        pltpu.SemaphoreType.REGULAR((4,)),
    ]
    operands = [
        pltpu.with_memory_space_constraint(value, pltpu.HBM)
        for value in (
            mode_shapes, span_stiff, chord_stiff, span_geo, chord_geo, ground, chord_len
        )
    ]
    in_hbm = pl.BlockSpec(memory_space=pltpu.HBM)
    shape = jax.ShapeDtypeStruct((M * D * R, C), f32)
    per_mode = jax.ShapeDtypeStruct((M * R, C), f32)
    in_vmem = pl.BlockSpec(memory_space=pltpu.VMEM)
    fields = pl.pallas_call(
        functools.partial(kernel, n_slab, n_sub, stages),
        out_shape=(shape,) * 5 + (per_mode,) * 2,
        in_specs=[in_hbm] * 7,
        out_specs=(in_vmem,) * 7,
        scratch_shapes=scratch,
        compiler_params=pltpu.CompilerParams(
            collective_id=0, has_side_effects=True, vmem_limit_bytes=24 << 20
        ),
    )(*operands)
    full = (M, D, R, C)
    r0, z0, q0, d0, image2 = [value.reshape(full) for value in fields[:5]]
    over, other = [value.reshape(M, 1, R, C) for value in fields[5:]]
    return z0 + over * z0 + other * d0, (r0 - q0) - over * q0 - other * image2


def solution(mesh):
    sizes = (mesh.shape["slab"], mesh.shape["sub"])
    return jax.shard_map(
        functools.partial(body, *sizes),
        mesh=mesh,
        in_specs=(
            P(None, None, "slab", "sub"),
            P(None, "slab", "sub"),
            P(None, "slab", "sub"),
            P("slab", "sub"),
            P("slab", "sub"),
            P(None, "slab", "sub"),
            P(),
        ),
        out_specs=(P(None, None, "slab", "sub"), P(None, None, "slab", "sub")),
        check_vma=False,
    )
```

```python
import functools

import jax
import jax.numpy as jnp
from jax import lax
from jax.experimental import pallas as pl
from jax.experimental.pallas import tpu as pltpu
from jax.sharding import PartitionSpec as P

MESH = pl.DeviceIdType.MESH
D = 6
R, C = 8, 128
M = 32
GROUPS = 2
GM = M // GROUPS
UNROLL = 16


def digits_of(n_slab):
    core = 2
    z = 16 if n_slab % 32 == 0 else 4 if n_slab % 8 == 0 else 1
    return core, z, n_slab // (core * z)


def digit_stages(n_slab, n_sub):
    core, z, y = digits_of(n_slab)
    return [[("slab", 1, core), ("sub", 1, n_sub), ("slab", core * z, y)], [("slab", core, z)]]


def stage_partners(digits, slab, sub):
    total = 1
    for _, _, size in digits:
        total *= size
    partners = []
    for offset in range(1, total):
        rest, at = offset, {"slab": slab, "sub": sub}
        for axis, stride, size in digits:
            step, rest = rest % size, rest // size
            digit = (at[axis] // stride) % size
            at[axis] = at[axis] + ((digit + step) % size - digit) * stride
        partners.append((at["slab"], at["sub"]))
    return partners


def total_of(terms):
    terms = list(terms)
    while len(terms) > 1:
        terms = [sum(terms[i : i + 2][1:], terms[i]) for i in range(0, len(terms), 2)]
    return terms[0]


def place(i, j):
    i, j = min(i, j), max(i, j)
    return i * D - i * (i - 1) // 2 + j - i


def kernel(
    n_slab,
    n_sub,
    stages,
    m_any,
    ss_any,
    cs_any,
    sg_any,
    cg_any,
    gr_any,
    len_any,
    r0,
    z0,
    q0,
    d0,
    image2,
    over,
    other,
    len_ref,
    m_in,
    ss,
    cs,
    sg,
    cg,
    gr,
    field,
    ssb,
    csb,
    fac,
    ts,
    us,
    tc,
    uc,
    prod,
    flip,
    coef_send,
    coef_span,
    coef_chord,
    row_first,
    row_last,
    from_ahead,
    from_behind,
    col_own,
    col_ahead,
    col_behind,
    w_ahead,
    w_behind,
    w_col,
    t_send,
    u_send,
    u_ahead,
    t_behind,
    tu_send,
    tu_ahead,
    tu_behind,
    *rest,
):
    parts = rest[: len(stages)]
    in_sem, send_sem, recv_sem, here_sem = rest[len(stages) :]
    slab, sub = lax.axis_index("slab"), lax.axis_index("sub")
    ahead = (lax.rem(slab + 1, n_slab), sub)
    behind = (lax.rem(slab + n_slab - 1, n_slab), sub)
    right = (slab, lax.rem(sub + 1, n_sub))
    left = (slab, lax.rem(sub + n_sub - 1, n_sub))
    partners = [stage_partners(digits, slab, sub) for digits in stages]

    loads = []
    for k, (source, target) in enumerate(
        ((m_any, m_in), (ss_any, ss), (cs_any, cs), (sg_any, sg), (cg_any, cg), (gr_any, gr), (len_any, len_ref))
    ):
        copy = pltpu.make_async_copy(source, target, in_sem.at[k])
        loads.append(copy)

    core, z_size, y_size = digits_of(n_slab)
    ring_x = stage_partners([("sub", 1, n_sub)], slab, sub)
    ring_y = stage_partners([("slab", core * z_size, y_size)], slab, sub)
    ring_z = stage_partners([("slab", core, z_size)], slab, sub)
    twin = stage_partners([("slab", 1, core)], slab, sub)

    def both_ways(ring, distance):
        return [ring[distance - 1], ring[len(ring) - distance]] if ring else []

    def tell(semaphore, devices):
        for device in devices:
            pl.semaphore_signal(semaphore, inc=1, device_id=device, device_id_type=MESH)

    barrier = pltpu.get_barrier_semaphore()
    greeted = [ahead, behind] + both_ways(ring_x, 1) + twin
    greeted += both_ways(ring_y, 1) + both_ways(ring_z, 1)
    tell(barrier, greeted)
    for copy in loads:
        copy.start()

    steps = [
        [both_ways(ring_x, 1), both_ways(ring_y, 1), both_ways(ring_y, 1), twin],
        [both_ways(ring_z, distance) for distance in (1, 2, 4) if 2 * distance < z_size],
    ]
    told = [0]

    def widen():
        for n, chain in enumerate(steps):
            if 0 < told[0] <= len(chain) and chain[told[0] - 1]:
                pl.semaphore_wait(here_sem.at[n, told[0] - 1], len(chain[told[0] - 1]))
            if told[0] < len(chain):
                tell(here_sem.at[n, told[0]], chain[told[0]])
        told[0] += 1

    row = lax.broadcasted_iota(jnp.int32, (R, C), 0)
    lane = lax.broadcasted_iota(jnp.int32, (R, C), 1)
    pair = lax.shift_right_logical(lane, 1)
    even = lane - 2 * pair == 0

    def tile(k):
        return pl.ds(pl.multiple_of(k * R, R), R)

    def wide(value):
        return jnp.broadcast_to(value, (R, C))

    def of_mode(ref, j):
        return [ref[tile(j * D + c), :] for c in range(D)]

    def keep(ref, j, vector):
        for c in range(D):
            ref[tile(j * D + c), :] = vector[c]

    def over_group(g, step, carry):
        def some(i, carry):
            for u in range(UNROLL):
                carry = step(g * GM + i * UNROLL + u, carry)
            return carry

        return lax.fori_loop(0, GM // UNROLL, some, carry)

    sent = []
    count = [0]

    def send(source, target, device):
        k = count[0]
        count[0] += 1
        copy = pltpu.make_async_remote_copy(
            src_ref=source,
            dst_ref=target,
            send_sem=send_sem.at[k],
            recv_sem=recv_sem.at[k],
            device_id=device,
            device_id_type=MESH,
        )
        copy.start()
        sent.append(copy)
        return copy

    loads[0].wait()

    def pack(i, packs):
        packs = list(packs)
        for u in range(UNROLL):
            j = i * UNROLL + u
            for c in range(D):
                value = m_in[j, c].astype(jnp.float32)
                field[tile(j * D + c), :] = value
                half = 32 * (c % 2)
                turned = pltpu.roll(value, 2 * (j + half) + 1, 1)
                packs[c // 2] = jnp.where(pair == j + half, turned, packs[c // 2])
        return tuple(packs)

    zero = jnp.zeros((R, C), jnp.float32)
    packs = lax.fori_loop(0, M // UNROLL, pack, (zero,) * 3)
    for v in range(3):
        col_own[pl.ds(v * R, R), :] = packs[v]
    for g in range(M // 8):
        for c in range(D):
            at = pl.ds((g * D + c) * 8, 8)
            row_first[at, :] = field[pl.ds((g * 8 * D + c) * R, 8, stride=D * R), :]
            row_last[at, :] = field[pl.ds((g * 8 * D + c) * R + R - 1, 8, stride=D * R), :]

    for copy in loads[1:]:
        copy.wait()
    span_coef, chord_coef = zero, zero
    for c in range(D + 1):
        mine = ss[c] if c < D else sg[...]
        span_coef = jnp.where(row == c, wide(mine[R - 1 :, :]), span_coef)
        mine = cs[c] if c < D else cg[...]
        chord_coef = jnp.where(lane == c, wide(mine[:, C - 1 :]), chord_coef)
    coef_send[0] = span_coef
    coef_send[1] = chord_coef

    pl.semaphore_wait(barrier, len(greeted))
    widen()
    got_coef = [
        send(coef_send.at[0], coef_span, ahead),
        send(coef_send.at[1], coef_chord, right),
    ]
    got_cols = [send(col_own, col_behind, right), send(col_own, col_ahead, left)]
    got_rows = []
    for g in range(M // 8):
        at = pl.ds(g * 8 * D, 8 * D)
        got_rows.append(
            [
                send(row_last.at[at], from_behind.at[at], ahead),
                send(row_first.at[at], from_ahead.at[at], behind),
            ]
        )

    n_stations = n_slab * R
    first = slab * R
    length = jnp.zeros((R, C), jnp.int32)
    length_next = jnp.zeros((R, C), jnp.int32)
    length_prev = jnp.zeros((R, C), jnp.int32)
    for k in range(-1, R + 1):
        here = len_ref[jnp.clip(first + k, 0, n_stations - 1)]
        if 0 <= k < R:
            length = jnp.where(row == k, here, length)
        if k >= 1:
            length_next = jnp.where(row == k - 1, here, length_next)
        if k < R - 1:
            length_prev = jnp.where(row == k + 1, here, length_prev)
    column = lane + sub * C
    station = row + first
    one = jnp.ones((R, C), jnp.float32)
    span_live = jnp.where(
        (column < length) & (column < length_next) & (station < n_stations - 1), one, zero
    )
    span_live_b = jnp.where(
        (column < length) & (column < length_prev) & (station > 0), one, zero
    )
    chord_live = jnp.where(column + 1 < length, one, zero)
    chord_live_b = jnp.where((column < length) & (column > 0), one, zero)
    span_geo = sg[...] * span_live
    chord_geo = cg[...] * chord_live

    sg[...] = span_geo
    cg[...] = chord_geo

    def weigh(j, carry):
        modes = of_mode(field, j)
        jumps = [pltpu.roll(value, R - 1, 0) - value for value in modes]
        ts[tile(j), :] = total_of(jump * jump for jump in jumps) * sg[...]
        jumps = [pltpu.roll(value, C - 1, 1) - value for value in modes]
        tc[tile(j), :] = total_of(jump * jump for jump in jumps) * cg[...]
        return carry

    for g in range(GROUPS):
        over_group(g, weigh, 0)

    for copy in got_coef:
        copy.wait_recv()
    widen()
    chord_ghost = coef_chord[...]
    for c in range(D):
        mine = ss[c]
        back = jnp.where(row == 0, wide(coef_span[pl.ds(c, 1), :]), pltpu.roll(mine, 1, 0))
        ssb[c] = back * span_live_b
        ss[c] = mine * span_live
        mine = cs[c]
        back = jnp.where(lane == 0, wide(chord_ghost[:, c : c + 1]), pltpu.roll(mine, 1, 1))
        csb[c] = back * chord_live_b
        cs[c] = mine * chord_live
    a_s = [ss[c] for c in range(D)]
    a_c = [cs[c] for c in range(D)]
    b_s = [ssb[c] for c in range(D)]
    b_c = [csb[c] for c in range(D)]
    low = [[None] * D for _ in range(D)]
    raw = [[None] * D for _ in range(D)]
    inverse = []
    for j in range(D):
        for i in range(j, D):
            entry = (a_s[i] * a_s[j] + b_s[i] * b_s[j]) + (a_c[i] * a_c[j] + b_c[i] * b_c[j])
            if i == j:
                entry = entry + gr[i]
            for n in range(j):
                entry = entry - raw[i][n] * low[j][n]
            raw[i][j] = entry
        inverse.append(1.0 / raw[j][j])
        for i in range(j + 1, D):
            low[i][j] = raw[i][j] * inverse[j]
    unit = [[None] * D for _ in range(D)]
    for j in range(D):
        for i in range(j + 1, D):
            entry = low[i][j]
            for n in range(j + 1, i):
                entry = entry + low[i][n] * unit[n][j]
            unit[i][j] = -entry
    scaled = [[None] * D for _ in range(D)]
    for k in range(D):
        for i in range(k):
            scaled[k][i] = unit[k][i] * inverse[k]
        scaled[k][k] = inverse[k]
    for i in range(D):
        for j in range(i, D):
            terms = [scaled[j][i] if i < j else inverse[j]]
            terms += [scaled[k][i] * unit[k][j] for k in range(j + 1, D)]
            fac[place(i, j)] = total_of(terms)

    def solve(vector):
        return [total_of(fac[place(i, j)] * vector[j] for j in range(D)) for i in range(D)]

    def dots(j, vector, packed):
        t_s = total_of(ss[c] * vector[c] for c in range(D))
        u_s = total_of(ssb[c] * vector[c] for c in range(D))
        t_c = total_of(cs[c] * vector[c] for c in range(D))
        u_c = total_of(csb[c] * vector[c] for c in range(D))
        ts[tile(j), :] = t_s
        us[tile(j), :] = u_s
        tc[tile(j), :] = t_c
        uc[tile(j), :] = u_c
        turned = pltpu.roll(jnp.where(lane == 0, u_c, t_c), 2 * j + 1, 1)
        return jnp.where(pair == j, turned, packed)

    def send_dots(turn, g, packed):
        at = pl.ds(turn * M + g * GM, GM)
        for b in range(GM // 8):
            from_mode = g * GM + b * 8
            to = pl.ds(turn * M + from_mode, 8)
            t_send[to, :] = ts[pl.ds(from_mode * R + R - 1, 8, stride=R), :]
            u_send[to, :] = us[pl.ds(from_mode * R, 8, stride=R), :]
        tu_send[turn, g] = packed
        return [
            send(t_send.at[at], t_behind.at[at], ahead),
            send(u_send.at[at], u_ahead.at[at], behind),
            send(tu_send.at[turn, g], tu_behind.at[turn, g], right),
            send(tu_send.at[turn, g], tu_ahead.at[turn, g], left),
        ]

    def edges_of(turn, g):
        return jnp.where(
            even,
            pltpu.roll(tu_ahead[turn, g], C - 1, 1),
            pltpu.roll(tu_behind[turn, g], 1, 1),
        )

    def operate(turn, j, vector, edge):
        t_s, u_s, t_c, u_c = ts[tile(j), :], us[tile(j), :], tc[tile(j), :], uc[tile(j), :]
        at = pl.ds(turn * M + j, 1)
        edge = pltpu.roll(edge, C - 1 - 2 * j, 1)
        u_s_next = jnp.where(row == R - 1, wide(u_ahead[at, :]), pltpu.roll(u_s, R - 1, 0))
        t_s_prev = jnp.where(row == 0, wide(t_behind[at, :]), pltpu.roll(t_s, 1, 0))
        u_c_next = jnp.where(lane == C - 1, edge, pltpu.roll(u_c, C - 1, 1))
        t_c_prev = jnp.where(lane == 0, edge, pltpu.roll(t_c, 1, 1))
        e_s, e_sb = u_s_next - t_s, u_s - t_s_prev
        e_c, e_cb = u_c_next - t_c, u_c - t_c_prev
        return [
            (gr[c] * vector[c] + (ssb[c] * e_sb - ss[c] * e_s)) + (csb[c] * e_cb - cs[c] * e_c)
            for c in range(D)
        ]

    for copy in got_cols:
        copy.wait_recv()
    square = None
    for v in range(3):
        at = pl.ds(v * R, R)
        across = jnp.where(
            even, pltpu.roll(col_ahead[at, :], C - 1, 1), pltpu.roll(col_behind[at, :], 1, 1)
        )
        jump = across - col_own[at, :]
        square = jump * jump if square is None else square + jump * jump
    square = square + pltpu.roll(square, C // 2, 1)
    geo_b = chord_ghost[:, D : D + 1] * chord_live_b[:, :1]
    w_col[...] = square * jnp.where(even, wide(chord_geo[:, C - 1 :]), wide(geo_b))
    geo_ahead = jnp.broadcast_to(span_geo[R - 1 :, :], (8, C))
    geo_behind = jnp.broadcast_to(coef_span[pl.ds(D, 1), :] * span_live_b[:1, :], (8, C))

    def load_step(j, packed):
        edge = pltpu.roll(w_col[...], C - 1 - 2 * j, 1)
        w_s = jnp.where(row == R - 1, wide(w_ahead[pl.ds(j, 1), :]), ts[tile(j), :])
        w_c = jnp.where(lane == C - 1, edge, tc[tile(j), :])
        w_sb = jnp.where(row == 0, wide(w_behind[pl.ds(j, 1), :]), pltpu.roll(w_s, 1, 0))
        w_cb = jnp.where(lane == 0, edge, pltpu.roll(w_c, 1, 1))
        load = [
            (ssb[c] * w_sb - ss[c] * w_s) + (csb[c] * w_cb - cs[c] * w_c) for c in range(D)
        ]
        first_z = solve(load)
        keep(r0, j, load)
        keep(z0, j, first_z)
        return dots(j, first_z, packed)

    widen()
    got_first = []
    for g in range(GROUPS):
        for b in range(GM // 8):
            block = g * (GM // 8) + b
            for copy in got_rows[block]:
                copy.wait_recv()
            to_ahead, to_behind = [], []
            for c in range(D):
                at = pl.ds((block * D + c) * 8, 8)
                jump = from_ahead[at, :] - row_last[at, :]
                to_ahead.append(jump * jump)
                jump = row_first[at, :] - from_behind[at, :]
                to_behind.append(jump * jump)
            w_ahead[pl.ds(block * 8, 8), :] = total_of(to_ahead) * geo_ahead
            w_behind[pl.ds(block * 8, 8), :] = total_of(to_behind) * geo_behind
        got_first.append(send_dots(0, g, over_group(g, load_step, zero)))

    def first_step(edge, j, packed):
        z = of_mode(z0, j)
        image = operate(0, j, z, edge)
        left_over = [a - b for a, b in zip(of_mode(r0, j), image)]
        second = solve(left_over)
        keep(q0, j, image)
        keep(d0, j, second)
        prod[tile(j), :] = total_of(a * b for a, b in zip(z, image))
        prod[tile(M + j), :] = total_of(a * b for a, b in zip(z, left_over))
        prod[tile(2 * M + j), :] = total_of(a * b for a, b in zip(second, left_over))
        return dots(j, second, packed)

    widen()
    got_second = []
    for g in range(GROUPS):
        for copy in got_first[g]:
            copy.wait_recv()
        edge = edges_of(0, g)
        packed = over_group(g, functools.partial(first_step, edge), zero)
        got_second.append(send_dots(1, g, packed))

    def fold(k):
        rows = [prod[pl.ds(k * 8 * R + n, 8, stride=R), :] for n in range(R)]
        flip[pl.ds(k * 8, 8), :] = total_of(rows)

    for k in range(3 * M // 8):
        fold(k)

    def second_step(edge, j, carry):
        second = of_mode(d0, j)
        image = operate(1, j, second, edge)
        keep(image2, j, image)
        prod[tile(3 * M + j), :] = total_of(a * b for a, b in zip(second, image))
        return carry

    widen()
    for g in range(GROUPS):
        for copy in got_second[g]:
            copy.wait_recv()
        over_group(g, functools.partial(second_step, edges_of(1, g)), 0)
    for k in range(3 * M // 8, 4 * M // 8):
        fold(k)

    while told[0] <= 4:
        widen()
    own = jnp.sum(jnp.transpose(flip[...]), axis=0, keepdims=True)
    for part, group in zip(parts, partners):
        members = len(group) + 1
        part[pl.ds(0, 1), :] = own
        copies = [
            send(part.at[pl.ds(0, 1)], part.at[pl.ds(n + 1, 1)], device)
            for n, device in enumerate(group)
        ]
        for copy in copies:
            copy.wait_recv()
        own = jnp.sum(part[pl.ds(0, members), :], axis=0, keepdims=True)

    zq = wide(own)
    zs = pltpu.roll(zq, C - M, 1)
    ds = pltpu.roll(zq, C - 2 * M, 1)
    dv = pltpu.roll(zq, C - 3 * M, 1)
    dq = zs - ds
    ratio = dq / zq
    second_part = (ds - dq * (zs / zq)) / (dv - ratio * dq)
    excess = (zs - dq * second_part) / zq

    def spread(j, carry):
        over[tile(j), :] = wide(pltpu.roll(excess, C - 1 - j, 1)[:, C - 1 :])
        other[tile(j), :] = wide(pltpu.roll(second_part, C - 1 - j, 1)[:, C - 1 :])
        return carry

    for g in range(GROUPS):
        over_group(g, spread, 0)
    for copy in sent:
        copy.wait_send()


def body(n_slab, n_sub, mode_shapes, span_stiff, chord_stiff, span_geo, chord_geo, ground, chord_len):
    stages = digit_stages(n_slab, n_sub)
    f32 = jnp.float32
    members = []
    for digits in stages:
        total = 1
        for _, _, size in digits:
            total *= size
        members.append(total)
    n_sends = 4 + 2 * (M // 8) + 8 * GROUPS + sum(members) - len(members)

    def big():
        return pltpu.VMEM((M * D * R, C), f32)

    rows = M * D
    scratch = [
        pltpu.SMEM(chord_len.shape, jnp.int32),
        pltpu.VMEM((M, D, R, C), jnp.bfloat16),
        pltpu.VMEM((D, R, C), f32),
        pltpu.VMEM((D, R, C), f32),
        pltpu.VMEM((R, C), f32),
        pltpu.VMEM((R, C), f32),
        pltpu.VMEM((D, R, C), f32),
        big(),
        pltpu.VMEM((D, R, C), f32),
        pltpu.VMEM((D, R, C), f32),
        pltpu.VMEM((21, R, C), f32),
        pltpu.VMEM((M * R, C), f32),
        pltpu.VMEM((M * R, C), f32),
        pltpu.VMEM((M * R, C), f32),
        pltpu.VMEM((M * R, C), f32),
        pltpu.VMEM((4 * M * R, C), f32),
        pltpu.VMEM((4 * M, C), f32),
        pltpu.VMEM((2, R, C), f32),
        pltpu.VMEM((R, C), f32),
        pltpu.VMEM((R, C), f32),
        pltpu.VMEM((rows, C), f32),
        pltpu.VMEM((rows, C), f32),
        pltpu.VMEM((rows, C), f32),
        pltpu.VMEM((rows, C), f32),
        pltpu.VMEM((3 * R, C), f32),
        pltpu.VMEM((3 * R, C), f32),
        pltpu.VMEM((3 * R, C), f32),
        pltpu.VMEM((M, C), f32),
        pltpu.VMEM((M, C), f32),
        pltpu.VMEM((R, C), f32),
        pltpu.VMEM((2 * M, C), f32),
        pltpu.VMEM((2 * M, C), f32),
        pltpu.VMEM((2 * M, C), f32),
        pltpu.VMEM((2 * M, C), f32),
        pltpu.VMEM((2, GROUPS, R, C), f32),
        pltpu.VMEM((2, GROUPS, R, C), f32),
        pltpu.VMEM((2, GROUPS, R, C), f32),
    ]
    scratch += [pltpu.VMEM((max(8, n), C), f32) for n in members]
    scratch += [
        pltpu.SemaphoreType.DMA((7,)),
        pltpu.SemaphoreType.DMA((n_sends,)),
        pltpu.SemaphoreType.DMA((n_sends,)),
        pltpu.SemaphoreType.REGULAR((2, 4)),
    ]
    operands = [
        pltpu.with_memory_space_constraint(value, pltpu.HBM)
        for value in (
            mode_shapes, span_stiff, chord_stiff, span_geo, chord_geo, ground, chord_len
        )
    ]
    in_hbm = pl.BlockSpec(memory_space=pltpu.HBM)
    shape = jax.ShapeDtypeStruct((M * D * R, C), f32)
    per_mode = jax.ShapeDtypeStruct((M * R, C), f32)
    in_vmem = pl.BlockSpec(memory_space=pltpu.VMEM)
    fields = pl.pallas_call(
        functools.partial(kernel, n_slab, n_sub, stages),
        out_shape=(shape,) * 5 + (per_mode,) * 2,
        in_specs=[in_hbm] * 7,
        out_specs=(in_vmem,) * 7,
        scratch_shapes=scratch,
        compiler_params=pltpu.CompilerParams(
            collective_id=0, has_side_effects=True, vmem_limit_bytes=24 << 20
        ),
    )(*operands)
    full = (M, D, R, C)
    r0, z0, q0, d0, image2 = [value.reshape(full) for value in fields[:5]]
    over, other = [value.reshape(M, 1, R, C) for value in fields[5:]]
    return z0 + over * z0 + other * d0, (r0 - q0) - over * q0 - other * image2


def solution(mesh):
    sizes = (mesh.shape["slab"], mesh.shape["sub"])
    return jax.shard_map(
        functools.partial(body, *sizes),
        mesh=mesh,
        in_specs=(
            P(None, None, "slab", "sub"),
            P(None, "slab", "sub"),
            P(None, "slab", "sub"),
            P("slab", "sub"),
            P("slab", "sub"),
            P(None, "slab", "sub"),
            P(),
        ),
        out_specs=(P(None, None, "slab", "sub"), P(None, None, "slab", "sub")),
        check_vma=False,
    )
```

```python
import functools

import jax
import jax.numpy as jnp
from jax import lax
from jax.experimental import pallas as pl
from jax.experimental.pallas import tpu as pltpu
from jax.sharding import PartitionSpec as P

MESH = pl.DeviceIdType.MESH
D = 6
R, C = 8, 128
M = 32
GROUPS = 2
GM = M // GROUPS
UNROLL = 16


def digits_of(n_slab):
    core = 2
    z = 16 if n_slab % 32 == 0 else 4 if n_slab % 8 == 0 else 1
    return core, z, n_slab // (core * z)


def digit_stages(n_slab, n_sub):
    core, z, y = digits_of(n_slab)
    return [[("slab", 1, core), ("sub", 1, n_sub), ("slab", core * z, y)], [("slab", core, z)]]


def stage_partners(digits, slab, sub):
    total = 1
    for _, _, size in digits:
        total *= size
    partners = []
    for offset in range(1, total):
        rest, at = offset, {"slab": slab, "sub": sub}
        for axis, stride, size in digits:
            step, rest = rest % size, rest // size
            digit = (at[axis] // stride) % size
            at[axis] = at[axis] + ((digit + step) % size - digit) * stride
        partners.append((at["slab"], at["sub"]))
    return partners


def total_of(terms):
    terms = list(terms)
    while len(terms) > 1:
        terms = [sum(terms[i : i + 2][1:], terms[i]) for i in range(0, len(terms), 2)]
    return terms[0]


def place(i, j):
    i, j = min(i, j), max(i, j)
    return i * D - i * (i - 1) // 2 + j - i


def kernel(
    n_slab,
    n_sub,
    stages,
    m_any,
    ss_any,
    cs_any,
    sg_any,
    cg_any,
    gr_any,
    len_any,
    r0,
    z0,
    q0,
    d0,
    image2,
    over,
    other,
    len_ref,
    m_in,
    ss,
    cs,
    sg,
    cg,
    gr,
    field,
    ssb,
    csb,
    edge_s,
    edge_c,
    back_s,
    back_c,
    cross,
    hs,
    hc,
    fac,
    ts,
    us,
    tc,
    uc,
    prod,
    flip,
    coef_send,
    coef_span,
    coef_chord,
    row_first,
    row_last,
    from_ahead,
    from_behind,
    col_own,
    col_ahead,
    col_behind,
    w_ahead,
    w_behind,
    w_col,
    t_send,
    u_send,
    u_ahead,
    t_behind,
    tu_send,
    tu_ahead,
    tu_behind,
    *rest,
):
    parts = rest[: len(stages)]
    in_sem, send_sem, recv_sem, here_sem = rest[len(stages) :]
    slab, sub = lax.axis_index("slab"), lax.axis_index("sub")
    ahead = (lax.rem(slab + 1, n_slab), sub)
    behind = (lax.rem(slab + n_slab - 1, n_slab), sub)
    right = (slab, lax.rem(sub + 1, n_sub))
    left = (slab, lax.rem(sub + n_sub - 1, n_sub))
    partners = [stage_partners(digits, slab, sub) for digits in stages]

    loads = []
    for k, (source, target) in enumerate(
        ((m_any, m_in), (ss_any, ss), (cs_any, cs), (sg_any, sg), (cg_any, cg), (gr_any, gr), (len_any, len_ref))
    ):
        copy = pltpu.make_async_copy(source, target, in_sem.at[k])
        loads.append(copy)

    core, z_size, y_size = digits_of(n_slab)
    ring_x = stage_partners([("sub", 1, n_sub)], slab, sub)
    ring_y = stage_partners([("slab", core * z_size, y_size)], slab, sub)
    ring_z = stage_partners([("slab", core, z_size)], slab, sub)
    twin = stage_partners([("slab", 1, core)], slab, sub)

    def both_ways(ring, distance):
        return [ring[distance - 1], ring[len(ring) - distance]] if ring else []

    def tell(semaphore, devices):
        for device in devices:
            pl.semaphore_signal(semaphore, inc=1, device_id=device, device_id_type=MESH)

    barrier = pltpu.get_barrier_semaphore()
    greeted = [ahead, behind] + both_ways(ring_x, 1) + twin
    greeted += both_ways(ring_y, 1) + both_ways(ring_z, 1)
    tell(barrier, greeted)
    for copy in loads:
        copy.start()

    steps = [
        [both_ways(ring_x, 1), both_ways(ring_y, 1), both_ways(ring_y, 1), twin],
        [both_ways(ring_z, distance) for distance in (1, 2, 4) if 2 * distance < z_size],
    ]
    told = [0]

    def widen():
        for n, chain in enumerate(steps):
            if 0 < told[0] <= len(chain) and chain[told[0] - 1]:
                pl.semaphore_wait(here_sem.at[n, told[0] - 1], len(chain[told[0] - 1]))
            if told[0] < len(chain):
                tell(here_sem.at[n, told[0]], chain[told[0]])
        told[0] += 1

    row = lax.broadcasted_iota(jnp.int32, (R, C), 0)
    lane = lax.broadcasted_iota(jnp.int32, (R, C), 1)
    pair = lax.shift_right_logical(lane, 1)
    even = lane - 2 * pair == 0

    def tile(k):
        return pl.ds(pl.multiple_of(k * R, R), R)

    def wide(value):
        return jnp.broadcast_to(value, (R, C))

    def of_mode(ref, j):
        return [ref[tile(j * D + c), :] for c in range(D)]

    def keep(ref, j, vector):
        for c in range(D):
            ref[tile(j * D + c), :] = vector[c]

    def over_group(g, step, carry):
        def some(i, carry):
            for u in range(UNROLL):
                carry = step(g * GM + i * UNROLL + u, carry)
            return carry

        return lax.fori_loop(0, GM // UNROLL, some, carry)

    sent = []
    count = [0]

    def send(source, target, device):
        k = count[0]
        count[0] += 1
        copy = pltpu.make_async_remote_copy(
            src_ref=source,
            dst_ref=target,
            send_sem=send_sem.at[k],
            recv_sem=recv_sem.at[k],
            device_id=device,
            device_id_type=MESH,
        )
        copy.start()
        sent.append(copy)
        return copy

    loads[0].wait()

    def pack(i, packs):
        packs = list(packs)
        for u in range(UNROLL):
            j = i * UNROLL + u
            for c in range(D):
                value = m_in[j, c].astype(jnp.float32)
                field[tile(j * D + c), :] = value
                half = 32 * (c % 2)
                turned = pltpu.roll(value, 2 * (j + half) + 1, 1)
                packs[c // 2] = jnp.where(pair == j + half, turned, packs[c // 2])
        return tuple(packs)

    zero = jnp.zeros((R, C), jnp.float32)
    packs = lax.fori_loop(0, M // UNROLL, pack, (zero,) * 3)
    for v in range(3):
        col_own[pl.ds(v * R, R), :] = packs[v]
    for g in range(M // 8):
        for c in range(D):
            at = pl.ds((g * D + c) * 8, 8)
            row_first[at, :] = field[pl.ds((g * 8 * D + c) * R, 8, stride=D * R), :]
            row_last[at, :] = field[pl.ds((g * 8 * D + c) * R + R - 1, 8, stride=D * R), :]

    for copy in loads[1:]:
        copy.wait()
    span_coef, chord_coef = zero, zero
    for c in range(D + 1):
        mine = ss[c] if c < D else sg[...]
        span_coef = jnp.where(row == c, wide(mine[R - 1 :, :]), span_coef)
        mine = cs[c] if c < D else cg[...]
        chord_coef = jnp.where(lane == c, wide(mine[:, C - 1 :]), chord_coef)
    coef_send[0] = span_coef
    coef_send[1] = chord_coef

    pl.semaphore_wait(barrier, len(greeted))
    widen()
    got_coef = [
        send(coef_send.at[0], coef_span, ahead),
        send(coef_send.at[1], coef_chord, right),
    ]
    got_cols = [send(col_own, col_behind, right), send(col_own, col_ahead, left)]
    got_rows = []
    for g in range(M // 8):
        at = pl.ds(g * 8 * D, 8 * D)
        got_rows.append(
            [
                send(row_last.at[at], from_behind.at[at], ahead),
                send(row_first.at[at], from_ahead.at[at], behind),
            ]
        )

    n_stations = n_slab * R
    first = slab * R
    length = jnp.zeros((R, C), jnp.int32)
    length_next = jnp.zeros((R, C), jnp.int32)
    length_prev = jnp.zeros((R, C), jnp.int32)
    for k in range(-1, R + 1):
        here = len_ref[jnp.clip(first + k, 0, n_stations - 1)]
        if 0 <= k < R:
            length = jnp.where(row == k, here, length)
        if k >= 1:
            length_next = jnp.where(row == k - 1, here, length_next)
        if k < R - 1:
            length_prev = jnp.where(row == k + 1, here, length_prev)
    column = lane + sub * C
    station = row + first
    one = jnp.ones((R, C), jnp.float32)
    span_live = jnp.where(
        (column < length) & (column < length_next) & (station < n_stations - 1), one, zero
    )
    span_live_b = jnp.where(
        (column < length) & (column < length_prev) & (station > 0), one, zero
    )
    chord_live = jnp.where(column + 1 < length, one, zero)
    chord_live_b = jnp.where((column < length) & (column > 0), one, zero)
    span_geo = sg[...] * span_live
    chord_geo = cg[...] * chord_live

    sg[...] = span_geo
    cg[...] = chord_geo

    def weigh(j, carry):
        modes = of_mode(field, j)
        jumps = [pltpu.roll(value, R - 1, 0) - value for value in modes]
        ts[tile(j), :] = total_of(jump * jump for jump in jumps) * sg[...]
        jumps = [pltpu.roll(value, C - 1, 1) - value for value in modes]
        tc[tile(j), :] = total_of(jump * jump for jump in jumps) * cg[...]
        return carry

    for g in range(GROUPS):
        over_group(g, weigh, 0)

    for copy in got_coef:
        copy.wait_recv()
    widen()
    chord_ghost = coef_chord[...]
    for c in range(D):
        mine = ss[c]
        back = jnp.where(row == 0, wide(coef_span[pl.ds(c, 1), :]), pltpu.roll(mine, 1, 0))
        ssb[c] = back * span_live_b
        ss[c] = mine * span_live
        mine = cs[c]
        back = jnp.where(lane == 0, wide(chord_ghost[:, c : c + 1]), pltpu.roll(mine, 1, 1))
        csb[c] = back * chord_live_b
        cs[c] = mine * chord_live
    a_s = [ss[c] for c in range(D)]
    a_c = [cs[c] for c in range(D)]
    b_s = [ssb[c] for c in range(D)]
    b_c = [csb[c] for c in range(D)]
    low = [[None] * D for _ in range(D)]
    raw = [[None] * D for _ in range(D)]
    inverse = []
    for j in range(D):
        for i in range(j, D):
            entry = (a_s[i] * a_s[j] + b_s[i] * b_s[j]) + (a_c[i] * a_c[j] + b_c[i] * b_c[j])
            if i == j:
                entry = entry + gr[i]
            for n in range(j):
                entry = entry - raw[i][n] * low[j][n]
            raw[i][j] = entry
        inverse.append(1.0 / raw[j][j])
        for i in range(j + 1, D):
            low[i][j] = raw[i][j] * inverse[j]
    unit = [[None] * D for _ in range(D)]
    for j in range(D):
        for i in range(j + 1, D):
            entry = low[i][j]
            for n in range(j + 1, i):
                entry = entry + low[i][n] * unit[n][j]
            unit[i][j] = -entry
    scaled = [[None] * D for _ in range(D)]
    for k in range(D):
        for i in range(k):
            scaled[k][i] = unit[k][i] * inverse[k]
        scaled[k][k] = inverse[k]
    for i in range(D):
        for j in range(i, D):
            terms = [scaled[j][i] if i < j else inverse[j]]
            terms += [scaled[k][i] * unit[k][j] for k in range(j + 1, D)]
            fac[place(i, j)] = total_of(terms)

    def solve(vector):
        return [total_of(fac[place(i, j)] * vector[j] for j in range(D)) for i in range(D)]

    def dots(vector):
        return [
            total_of(coef[c] * vector[c] for c in range(D)) for coef in (ss, ssb, cs, csb)
        ]

    def keep_dots(j, values):
        for ref, value in zip((ts, us, tc, uc), values):
            ref[tile(j), :] = value

    def kept_dots(j):
        return [ref[tile(j), :] for ref in (ts, us, tc, uc)]

    def pack_dots(j, values, packed):
        turned = pltpu.roll(jnp.where(lane == 0, values[3], values[2]), 2 * j + 1, 1)
        return jnp.where(pair == j, turned, packed)

    def send_dots(turn, g, packed):
        at = pl.ds(turn * M + g * GM, GM)
        for b in range(GM // 8):
            from_mode = g * GM + b * 8
            to = pl.ds(turn * M + from_mode, 8)
            t_send[to, :] = ts[pl.ds(from_mode * R + R - 1, 8, stride=R), :]
            u_send[to, :] = us[pl.ds(from_mode * R, 8, stride=R), :]
        tu_send[turn, g] = packed
        return [
            send(t_send.at[at], t_behind.at[at], ahead),
            send(u_send.at[at], u_ahead.at[at], behind),
            send(tu_send.at[turn, g], tu_behind.at[turn, g], right),
            send(tu_send.at[turn, g], tu_ahead.at[turn, g], left),
        ]

    def edges_of(turn, g):
        return jnp.where(
            even,
            pltpu.roll(tu_ahead[turn, g], C - 1, 1),
            pltpu.roll(tu_behind[turn, g], 1, 1),
        )

    def operate(vector, values):
        t_s, u_s, t_c, u_c = values
        u_s_next = jnp.where(row == R - 1, 0.0, pltpu.roll(u_s, R - 1, 0))
        t_s_prev = jnp.where(row == 0, 0.0, pltpu.roll(t_s, 1, 0))
        u_c_next = jnp.where(lane == C - 1, 0.0, pltpu.roll(u_c, C - 1, 1))
        t_c_prev = jnp.where(lane == 0, 0.0, pltpu.roll(t_c, 1, 1))
        e_s, e_sb = u_s_next - t_s, u_s - t_s_prev
        e_c, e_cb = u_c_next - t_c, u_c - t_c_prev
        return [
            (gr[c] * vector[c] + (ssb[c] * e_sb - ss[c] * e_s)) + (csb[c] * e_cb - cs[c] * e_c)
            for c in range(D)
        ]

    def arrived(turn, j, edge):
        at = pl.ds(turn * M + j, 1)
        along_s = jnp.where(row == 0, wide(t_behind[at, :]), wide(u_ahead[at, :]))
        along_c = pltpu.roll(edge, C - 1 - 2 * j, 1)
        hs[tile(j), :] = along_s
        hc[tile(j), :] = along_c
        return along_s, along_c

    for copy in got_cols:
        copy.wait_recv()
    square = None
    for v in range(3):
        at = pl.ds(v * R, R)
        across = jnp.where(
            even, pltpu.roll(col_ahead[at, :], C - 1, 1), pltpu.roll(col_behind[at, :], 1, 1)
        )
        jump = across - col_own[at, :]
        square = jump * jump if square is None else square + jump * jump
    square = square + pltpu.roll(square, C // 2, 1)
    geo_b = chord_ghost[:, D : D + 1] * chord_live_b[:, :1]
    w_col[...] = square * jnp.where(even, wide(chord_geo[:, C - 1 :]), wide(geo_b))
    geo_ahead = jnp.broadcast_to(span_geo[R - 1 :, :], (8, C))
    geo_behind = jnp.broadcast_to(coef_span[pl.ds(D, 1), :] * span_live_b[:1, :], (8, C))

    def load_step(j, packed):
        edge = pltpu.roll(w_col[...], C - 1 - 2 * j, 1)
        w_s = jnp.where(row == R - 1, wide(w_ahead[pl.ds(j, 1), :]), ts[tile(j), :])
        w_c = jnp.where(lane == C - 1, edge, tc[tile(j), :])
        w_sb = jnp.where(row == 0, wide(w_behind[pl.ds(j, 1), :]), pltpu.roll(w_s, 1, 0))
        w_cb = jnp.where(lane == 0, edge, pltpu.roll(w_c, 1, 1))
        load = [
            (ssb[c] * w_sb - ss[c] * w_s) + (csb[c] * w_cb - cs[c] * w_c) for c in range(D)
        ]
        first_z = solve(load)
        keep(r0, j, load)
        keep(z0, j, first_z)
        values = dots(first_z)
        keep_dots(j, values)
        return pack_dots(j, values, packed)

    widen()
    got_first = []
    for g in range(GROUPS):
        for b in range(GM // 8):
            block = g * (GM // 8) + b
            for copy in got_rows[block]:
                copy.wait_recv()
            to_ahead, to_behind = [], []
            for c in range(D):
                at = pl.ds((block * D + c) * 8, 8)
                jump = from_ahead[at, :] - row_last[at, :]
                to_ahead.append(jump * jump)
                jump = row_first[at, :] - from_behind[at, :]
                to_behind.append(jump * jump)
            w_ahead[pl.ds(block * 8, 8), :] = total_of(to_ahead) * geo_ahead
            w_behind[pl.ds(block * 8, 8), :] = total_of(to_behind) * geo_behind
        got_first.append(send_dots(0, g, over_group(g, load_step, zero)))

    for c in range(D):
        edge_s[c] = jnp.where(row == R - 1, ss[c], jnp.where(row == 0, ssb[c], 0.0))
        edge_c[c] = jnp.where(lane == C - 1, cs[c], jnp.where(lane == 0, csb[c], 0.0))
    for source, target in ((edge_s, back_s), (edge_c, back_c)):
        for c, value in enumerate(solve([source[c] for c in range(D)])):
            target[c] = value
    for n, source in enumerate((back_s, back_c)):
        for k, value in enumerate(dots([source[c] for c in range(D)])):
            cross[2 * k + n] = value

    def base_step(j, carry):
        z = of_mode(z0, j)
        image = operate(z, kept_dots(j))
        second = solve([a - b for a, b in zip(of_mode(r0, j), image)])
        keep(q0, j, image)
        keep(d0, j, second)
        keep_dots(j, dots(second))
        return carry

    for g in range(GROUPS):
        over_group(g, base_step, 0)
    widen()

    def first_step(edge, j, packed):
        along_s, along_c = arrived(0, j, edge)
        values = [
            value + (cross[2 * k] * along_s + cross[2 * k + 1] * along_c)
            for k, value in enumerate(kept_dots(j))
        ]
        keep_dots(j, values)
        return pack_dots(j, values, packed)

    got_second = []
    for g in range(GROUPS):
        for copy in got_first[g]:
            copy.wait_recv()
        packed = over_group(g, functools.partial(first_step, edges_of(0, g)), zero)
        got_second.append(send_dots(1, g, packed))

    def finish_step(j, carry):
        along_s, along_c = hs[tile(j), :], hc[tile(j), :]
        z, image, second = of_mode(z0, j), of_mode(q0, j), of_mode(d0, j)
        image = [
            value - (edge_s[c] * along_s + edge_c[c] * along_c) for c, value in enumerate(image)
        ]
        second = [
            value + (back_s[c] * along_s + back_c[c] * along_c) for c, value in enumerate(second)
        ]
        left_over = [a - b for a, b in zip(of_mode(r0, j), image)]
        keep(q0, j, image)
        keep(d0, j, second)
        prod[tile(j), :] = total_of(a * b for a, b in zip(z, image))
        prod[tile(M + j), :] = total_of(a * b for a, b in zip(z, left_over))
        prod[tile(2 * M + j), :] = total_of(a * b for a, b in zip(second, left_over))
        image = operate(second, kept_dots(j))
        keep(image2, j, image)
        prod[tile(3 * M + j), :] = total_of(a * b for a, b in zip(second, image))
        return carry

    for g in range(GROUPS):
        over_group(g, finish_step, 0)

    def fold(k):
        rows = [prod[pl.ds(k * 8 * R + n, 8, stride=R), :] for n in range(R)]
        flip[pl.ds(k * 8, 8), :] = total_of(rows)

    for k in range(3 * M // 8):
        fold(k)
    widen()

    def second_step(edge, j, carry):
        along_s, along_c = arrived(1, j, edge)
        t_s, u_s, t_c, u_c = kept_dots(j)
        change = jnp.where(row == R - 1, t_s, jnp.where(row == 0, u_s, 0.0)) * along_s
        change = change + (
            jnp.where(lane == C - 1, t_c, jnp.where(lane == 0, u_c, 0.0)) * along_c
        )
        prod[tile(3 * M + j), :] = prod[tile(3 * M + j), :] - change
        return carry

    for g in range(GROUPS):
        for copy in got_second[g]:
            copy.wait_recv()
        over_group(g, functools.partial(second_step, edges_of(1, g)), 0)
    for k in range(3 * M // 8, 4 * M // 8):
        fold(k)

    def last_image(j, carry):
        along_s, along_c = hs[tile(j), :], hc[tile(j), :]
        for c in range(D):
            at = tile(j * D + c)
            image2[at, :] = image2[at, :] - (edge_s[c] * along_s + edge_c[c] * along_c)
        return carry

    while told[0] <= 4:
        widen()
    own = jnp.sum(jnp.transpose(flip[...]), axis=0, keepdims=True)
    for part, group in zip(parts, partners):
        members = len(group) + 1
        part[pl.ds(0, 1), :] = own
        copies = [
            send(part.at[pl.ds(0, 1)], part.at[pl.ds(n + 1, 1)], device)
            for n, device in enumerate(group)
        ]
        if part is parts[0]:
            for g in range(GROUPS):
                over_group(g, last_image, 0)
        for copy in copies:
            copy.wait_recv()
        own = jnp.sum(part[pl.ds(0, members), :], axis=0, keepdims=True)

    zq = wide(own)
    zs = pltpu.roll(zq, C - M, 1)
    ds = pltpu.roll(zq, C - 2 * M, 1)
    dv = pltpu.roll(zq, C - 3 * M, 1)
    dq = zs - ds
    ratio = dq / zq
    second_part = (ds - dq * (zs / zq)) / (dv - ratio * dq)
    excess = (zs - dq * second_part) / zq

    def spread(j, carry):
        over[tile(j), :] = wide(pltpu.roll(excess, C - 1 - j, 1)[:, C - 1 :])
        other[tile(j), :] = wide(pltpu.roll(second_part, C - 1 - j, 1)[:, C - 1 :])
        return carry

    for g in range(GROUPS):
        over_group(g, spread, 0)
    for copy in sent:
        copy.wait_send()


def body(n_slab, n_sub, mode_shapes, span_stiff, chord_stiff, span_geo, chord_geo, ground, chord_len):
    stages = digit_stages(n_slab, n_sub)
    f32 = jnp.float32
    members = []
    for digits in stages:
        total = 1
        for _, _, size in digits:
            total *= size
        members.append(total)
    n_sends = 4 + 2 * (M // 8) + 8 * GROUPS + sum(members) - len(members)

    def big():
        return pltpu.VMEM((M * D * R, C), f32)

    rows = M * D
    scratch = [
        pltpu.SMEM(chord_len.shape, jnp.int32),
        pltpu.VMEM((M, D, R, C), jnp.bfloat16),
        pltpu.VMEM((D, R, C), f32),
        pltpu.VMEM((D, R, C), f32),
        pltpu.VMEM((R, C), f32),
        pltpu.VMEM((R, C), f32),
        pltpu.VMEM((D, R, C), f32),
        big(),
        pltpu.VMEM((D, R, C), f32),
        pltpu.VMEM((D, R, C), f32),
        pltpu.VMEM((D, R, C), f32),
        pltpu.VMEM((D, R, C), f32),
        pltpu.VMEM((D, R, C), f32),
        pltpu.VMEM((D, R, C), f32),
        pltpu.VMEM((8, R, C), f32),
        pltpu.VMEM((M * R, C), f32),
        pltpu.VMEM((M * R, C), f32),
        pltpu.VMEM((21, R, C), f32),
        pltpu.VMEM((M * R, C), f32),
        pltpu.VMEM((M * R, C), f32),
        pltpu.VMEM((M * R, C), f32),
        pltpu.VMEM((M * R, C), f32),
        pltpu.VMEM((4 * M * R, C), f32),
        pltpu.VMEM((4 * M, C), f32),
        pltpu.VMEM((2, R, C), f32),
        pltpu.VMEM((R, C), f32),
        pltpu.VMEM((R, C), f32),
        pltpu.VMEM((rows, C), f32),
        pltpu.VMEM((rows, C), f32),
        pltpu.VMEM((rows, C), f32),
        pltpu.VMEM((rows, C), f32),
        pltpu.VMEM((3 * R, C), f32),
        pltpu.VMEM((3 * R, C), f32),
        pltpu.VMEM((3 * R, C), f32),
        pltpu.VMEM((M, C), f32),
        pltpu.VMEM((M, C), f32),
        pltpu.VMEM((R, C), f32),
        pltpu.VMEM((2 * M, C), f32),
        pltpu.VMEM((2 * M, C), f32),
        pltpu.VMEM((2 * M, C), f32),
        pltpu.VMEM((2 * M, C), f32),
        pltpu.VMEM((2, GROUPS, R, C), f32),
        pltpu.VMEM((2, GROUPS, R, C), f32),
        pltpu.VMEM((2, GROUPS, R, C), f32),
    ]
    scratch += [pltpu.VMEM((max(8, n), C), f32) for n in members]
    scratch += [
        pltpu.SemaphoreType.DMA((7,)),
        pltpu.SemaphoreType.DMA((n_sends,)),
        pltpu.SemaphoreType.DMA((n_sends,)),
        pltpu.SemaphoreType.REGULAR((2, 4)),
    ]
    operands = [
        pltpu.with_memory_space_constraint(value, pltpu.HBM)
        for value in (
            mode_shapes, span_stiff, chord_stiff, span_geo, chord_geo, ground, chord_len
        )
    ]
    in_hbm = pl.BlockSpec(memory_space=pltpu.HBM)
    shape = jax.ShapeDtypeStruct((M * D * R, C), f32)
    per_mode = jax.ShapeDtypeStruct((M * R, C), f32)
    in_vmem = pl.BlockSpec(memory_space=pltpu.VMEM)
    fields = pl.pallas_call(
        functools.partial(kernel, n_slab, n_sub, stages),
        out_shape=(shape,) * 5 + (per_mode,) * 2,
        in_specs=[in_hbm] * 7,
        out_specs=(in_vmem,) * 7,
        scratch_shapes=scratch,
        compiler_params=pltpu.CompilerParams(
            collective_id=0, has_side_effects=True, vmem_limit_bytes=24 << 20
        ),
    )(*operands)
    full = (M, D, R, C)
    r0, z0, q0, d0, image2 = [value.reshape(full) for value in fields[:5]]
    over, other = [value.reshape(M, 1, R, C) for value in fields[5:]]
    return z0 + over * z0 + other * d0, (r0 - q0) - over * q0 - other * image2


def solution(mesh):
    sizes = (mesh.shape["slab"], mesh.shape["sub"])
    return jax.shard_map(
        functools.partial(body, *sizes),
        mesh=mesh,
        in_specs=(
            P(None, None, "slab", "sub"),
            P(None, "slab", "sub"),
            P(None, "slab", "sub"),
            P("slab", "sub"),
            P("slab", "sub"),
            P(None, "slab", "sub"),
            P(),
        ),
        out_specs=(P(None, None, "slab", "sub"), P(None, None, "slab", "sub")),
        check_vma=False,
    )
```

```python
import functools

import jax
import jax.numpy as jnp
from jax import lax
from jax.experimental import pallas as pl
from jax.experimental.pallas import tpu as pltpu
from jax.sharding import PartitionSpec as P

MESH = pl.DeviceIdType.MESH
D = 6
R, C = 8, 128
M = 32
GROUPS = 2
GM = M // GROUPS
UNROLL = 16


def digits_of(n_slab):
    core = 2
    z = 16 if n_slab % 32 == 0 else 4 if n_slab % 8 == 0 else 1
    return core, z, n_slab // (core * z)


def digit_stages(n_slab, n_sub):
    core, z, y = digits_of(n_slab)
    return [[("slab", 1, core), ("sub", 1, n_sub), ("slab", core * z, y)], [("slab", core, z)]]


def stage_partners(digits, slab, sub):
    total = 1
    for _, _, size in digits:
        total *= size
    partners = []
    for offset in range(1, total):
        rest, at = offset, {"slab": slab, "sub": sub}
        for axis, stride, size in digits:
            step, rest = rest % size, rest // size
            digit = (at[axis] // stride) % size
            at[axis] = at[axis] + ((digit + step) % size - digit) * stride
        partners.append((at["slab"], at["sub"]))
    return partners


def total_of(terms):
    terms = list(terms)
    while len(terms) > 1:
        terms = [sum(terms[i : i + 2][1:], terms[i]) for i in range(0, len(terms), 2)]
    return terms[0]


def place(i, j):
    i, j = min(i, j), max(i, j)
    return i * D - i * (i - 1) // 2 + j - i


def kernel(
    n_slab,
    n_sub,
    stages,
    m_any,
    ss_any,
    cs_any,
    sg_any,
    cg_any,
    gr_any,
    len_any,
    r0,
    z0,
    q0,
    d0,
    image2,
    over,
    other,
    len_ref,
    m_in,
    ss,
    cs,
    sg,
    cg,
    gr,
    field,
    ssb,
    csb,
    edge_s,
    edge_c,
    back_s,
    back_c,
    cross,
    hs,
    hc,
    fac,
    ts,
    us,
    tc,
    uc,
    prod,
    flip,
    coef_send,
    coef_span,
    coef_chord,
    row_first,
    row_last,
    from_ahead,
    from_behind,
    col_own,
    col_ahead,
    col_behind,
    w_ahead,
    w_behind,
    w_col,
    t_send,
    u_send,
    u_ahead,
    t_behind,
    tu_send,
    tu_ahead,
    tu_behind,
    *rest,
):
    parts = rest[: len(stages)]
    in_sem, send_sem, recv_sem, here_sem = rest[len(stages) :]
    slab, sub = lax.axis_index("slab"), lax.axis_index("sub")
    ahead = (lax.rem(slab + 1, n_slab), sub)
    behind = (lax.rem(slab + n_slab - 1, n_slab), sub)
    right = (slab, lax.rem(sub + 1, n_sub))
    left = (slab, lax.rem(sub + n_sub - 1, n_sub))
    partners = [stage_partners(digits, slab, sub) for digits in stages]

    loads = []
    for k, (source, target) in enumerate(
        ((m_any, m_in), (ss_any, ss), (cs_any, cs), (sg_any, sg), (cg_any, cg), (gr_any, gr), (len_any, len_ref))
    ):
        copy = pltpu.make_async_copy(source, target, in_sem.at[k])
        loads.append(copy)

    core, z_size, y_size = digits_of(n_slab)
    ring_x = stage_partners([("sub", 1, n_sub)], slab, sub)
    ring_y = stage_partners([("slab", core * z_size, y_size)], slab, sub)
    ring_z = stage_partners([("slab", core, z_size)], slab, sub)
    twin = stage_partners([("slab", 1, core)], slab, sub)

    def both_ways(ring, distance):
        return [ring[distance - 1], ring[len(ring) - distance]] if ring else []

    def tell(semaphore, devices):
        for device in devices:
            pl.semaphore_signal(semaphore, inc=1, device_id=device, device_id_type=MESH)

    barrier = pltpu.get_barrier_semaphore()
    greeted = [ahead, behind] + both_ways(ring_x, 1) + twin
    greeted += both_ways(ring_y, 1) + both_ways(ring_z, 1)
    tell(barrier, greeted)
    for copy in loads:
        copy.start()

    steps = [
        [both_ways(ring_x, 1), both_ways(ring_y, 1), both_ways(ring_y, 1), twin],
        [both_ways(ring_z, distance) for distance in (1, 2, 4) if 2 * distance < z_size],
    ]
    told = [0, 0]

    def widen(n):
        chain, step = steps[n], told[n]
        if 0 < step <= len(chain) and chain[step - 1]:
            pl.semaphore_wait(here_sem.at[n, step - 1], len(chain[step - 1]))
        if step < len(chain):
            tell(here_sem.at[n, step], chain[step])
        told[n] += 1

    row = lax.broadcasted_iota(jnp.int32, (R, C), 0)
    lane = lax.broadcasted_iota(jnp.int32, (R, C), 1)
    pair = lax.shift_right_logical(lane, 1)
    even = lane - 2 * pair == 0

    def tile(k):
        return pl.ds(pl.multiple_of(k * R, R), R)

    def wide(value):
        return jnp.broadcast_to(value, (R, C))

    def of_mode(ref, j):
        return [ref[tile(j * D + c), :] for c in range(D)]

    def keep(ref, j, vector):
        for c in range(D):
            ref[tile(j * D + c), :] = vector[c]

    def over_group(g, step, carry):
        def some(i, carry):
            for u in range(UNROLL):
                carry = step(g * GM + i * UNROLL + u, carry)
            return carry

        return lax.fori_loop(0, GM // UNROLL, some, carry)

    sent = []
    count = [0]

    def send(source, target, device):
        k = count[0]
        count[0] += 1
        copy = pltpu.make_async_remote_copy(
            src_ref=source,
            dst_ref=target,
            send_sem=send_sem.at[k],
            recv_sem=recv_sem.at[k],
            device_id=device,
            device_id_type=MESH,
        )
        copy.start()
        sent.append(copy)
        return copy

    loads[0].wait()

    def pack(i, packs):
        packs = list(packs)
        for u in range(UNROLL):
            j = i * UNROLL + u
            for c in range(D):
                value = m_in[j, c].astype(jnp.float32)
                field[tile(j * D + c), :] = value
                half = 32 * (c % 2)
                turned = pltpu.roll(value, 2 * (j + half) + 1, 1)
                packs[c // 2] = jnp.where(pair == j + half, turned, packs[c // 2])
        return tuple(packs)

    zero = jnp.zeros((R, C), jnp.float32)
    packs = lax.fori_loop(0, M // UNROLL, pack, (zero,) * 3)
    for v in range(3):
        col_own[pl.ds(v * R, R), :] = packs[v]
    for g in range(M // 8):
        for c in range(D):
            at = pl.ds((g * D + c) * 8, 8)
            row_first[at, :] = field[pl.ds((g * 8 * D + c) * R, 8, stride=D * R), :]
            row_last[at, :] = field[pl.ds((g * 8 * D + c) * R + R - 1, 8, stride=D * R), :]

    for copy in loads[1:]:
        copy.wait()
    span_coef, chord_coef = zero, zero
    for c in range(D + 1):
        mine = ss[c] if c < D else sg[...]
        span_coef = jnp.where(row == c, wide(mine[R - 1 :, :]), span_coef)
        mine = cs[c] if c < D else cg[...]
        chord_coef = jnp.where(lane == c, wide(mine[:, C - 1 :]), chord_coef)
    coef_send[0] = span_coef
    coef_send[1] = chord_coef

    pl.semaphore_wait(barrier, len(greeted))
    widen(0)
    widen(1)
    got_coef = [
        send(coef_send.at[0], coef_span, ahead),
        send(coef_send.at[1], coef_chord, right),
    ]
    got_cols = [send(col_own, col_behind, right), send(col_own, col_ahead, left)]
    got_rows = []
    for g in range(M // 8):
        at = pl.ds(g * 8 * D, 8 * D)
        got_rows.append(
            [
                send(row_last.at[at], from_behind.at[at], ahead),
                send(row_first.at[at], from_ahead.at[at], behind),
            ]
        )

    n_stations = n_slab * R
    first = slab * R
    length = jnp.zeros((R, C), jnp.int32)
    length_next = jnp.zeros((R, C), jnp.int32)
    length_prev = jnp.zeros((R, C), jnp.int32)
    for k in range(-1, R + 1):
        here = len_ref[jnp.clip(first + k, 0, n_stations - 1)]
        if 0 <= k < R:
            length = jnp.where(row == k, here, length)
        if k >= 1:
            length_next = jnp.where(row == k - 1, here, length_next)
        if k < R - 1:
            length_prev = jnp.where(row == k + 1, here, length_prev)
    column = lane + sub * C
    station = row + first
    one = jnp.ones((R, C), jnp.float32)
    span_live = jnp.where(
        (column < length) & (column < length_next) & (station < n_stations - 1), one, zero
    )
    span_live_b = jnp.where(
        (column < length) & (column < length_prev) & (station > 0), one, zero
    )
    chord_live = jnp.where(column + 1 < length, one, zero)
    chord_live_b = jnp.where((column < length) & (column > 0), one, zero)
    span_geo = sg[...] * span_live
    chord_geo = cg[...] * chord_live

    sg[...] = span_geo
    cg[...] = chord_geo

    def weigh(j, carry):
        modes = of_mode(field, j)
        jumps = [pltpu.roll(value, R - 1, 0) - value for value in modes]
        ts[tile(j), :] = total_of(jump * jump for jump in jumps) * sg[...]
        jumps = [pltpu.roll(value, C - 1, 1) - value for value in modes]
        tc[tile(j), :] = total_of(jump * jump for jump in jumps) * cg[...]
        return carry

    for g in range(GROUPS):
        over_group(g, weigh, 0)

    for copy in got_coef:
        copy.wait_recv()
    widen(0)
    widen(1)
    chord_ghost = coef_chord[...]
    for c in range(D):
        mine = ss[c]
        back = jnp.where(row == 0, wide(coef_span[pl.ds(c, 1), :]), pltpu.roll(mine, 1, 0))
        ssb[c] = back * span_live_b
        ss[c] = mine * span_live
        mine = cs[c]
        back = jnp.where(lane == 0, wide(chord_ghost[:, c : c + 1]), pltpu.roll(mine, 1, 1))
        csb[c] = back * chord_live_b
        cs[c] = mine * chord_live
    a_s = [ss[c] for c in range(D)]
    a_c = [cs[c] for c in range(D)]
    b_s = [ssb[c] for c in range(D)]
    b_c = [csb[c] for c in range(D)]
    low = [[None] * D for _ in range(D)]
    raw = [[None] * D for _ in range(D)]
    inverse = []
    for j in range(D):
        for i in range(j, D):
            entry = (a_s[i] * a_s[j] + b_s[i] * b_s[j]) + (a_c[i] * a_c[j] + b_c[i] * b_c[j])
            if i == j:
                entry = entry + gr[i]
            for n in range(j):
                entry = entry - raw[i][n] * low[j][n]
            raw[i][j] = entry
        inverse.append(1.0 / raw[j][j])
        for i in range(j + 1, D):
            low[i][j] = raw[i][j] * inverse[j]
    unit = [[None] * D for _ in range(D)]
    for j in range(D):
        for i in range(j + 1, D):
            entry = low[i][j]
            for n in range(j + 1, i):
                entry = entry + low[i][n] * unit[n][j]
            unit[i][j] = -entry
    scaled = [[None] * D for _ in range(D)]
    for k in range(D):
        for i in range(k):
            scaled[k][i] = unit[k][i] * inverse[k]
        scaled[k][k] = inverse[k]
    for i in range(D):
        for j in range(i, D):
            terms = [scaled[j][i] if i < j else inverse[j]]
            terms += [scaled[k][i] * unit[k][j] for k in range(j + 1, D)]
            fac[place(i, j)] = total_of(terms)

    def solve(vector):
        return [total_of(fac[place(i, j)] * vector[j] for j in range(D)) for i in range(D)]

    def dots(vector):
        return [
            total_of(coef[c] * vector[c] for c in range(D)) for coef in (ss, ssb, cs, csb)
        ]

    def keep_dots(j, values):
        for ref, value in zip((ts, us, tc, uc), values):
            ref[tile(j), :] = value

    def kept_dots(j):
        return [ref[tile(j), :] for ref in (ts, us, tc, uc)]

    def pack_dots(j, values, packed):
        turned = pltpu.roll(jnp.where(lane == 0, values[3], values[2]), 2 * j + 1, 1)
        return jnp.where(pair == j, turned, packed)

    def send_dots(turn, g, packed):
        at = pl.ds(turn * M + g * GM, GM)
        for b in range(GM // 8):
            from_mode = g * GM + b * 8
            to = pl.ds(turn * M + from_mode, 8)
            t_send[to, :] = ts[pl.ds(from_mode * R + R - 1, 8, stride=R), :]
            u_send[to, :] = us[pl.ds(from_mode * R, 8, stride=R), :]
        tu_send[turn, g] = packed
        return [
            send(t_send.at[at], t_behind.at[at], ahead),
            send(u_send.at[at], u_ahead.at[at], behind),
            send(tu_send.at[turn, g], tu_behind.at[turn, g], right),
            send(tu_send.at[turn, g], tu_ahead.at[turn, g], left),
        ]

    def edges_of(turn, g):
        return jnp.where(
            even,
            pltpu.roll(tu_ahead[turn, g], C - 1, 1),
            pltpu.roll(tu_behind[turn, g], 1, 1),
        )

    def operate(vector, values):
        t_s, u_s, t_c, u_c = values
        u_s_next = jnp.where(row == R - 1, 0.0, pltpu.roll(u_s, R - 1, 0))
        t_s_prev = jnp.where(row == 0, 0.0, pltpu.roll(t_s, 1, 0))
        u_c_next = jnp.where(lane == C - 1, 0.0, pltpu.roll(u_c, C - 1, 1))
        t_c_prev = jnp.where(lane == 0, 0.0, pltpu.roll(t_c, 1, 1))
        e_s, e_sb = u_s_next - t_s, u_s - t_s_prev
        e_c, e_cb = u_c_next - t_c, u_c - t_c_prev
        return [
            (gr[c] * vector[c] + (ssb[c] * e_sb - ss[c] * e_s)) + (csb[c] * e_cb - cs[c] * e_c)
            for c in range(D)
        ]

    def arrived(turn, j, edge):
        at = pl.ds(turn * M + j, 1)
        along_s = jnp.where(row == 0, wide(t_behind[at, :]), wide(u_ahead[at, :]))
        along_c = pltpu.roll(edge, C - 1 - 2 * j, 1)
        hs[tile(j), :] = along_s
        hc[tile(j), :] = along_c
        return along_s, along_c

    for copy in got_cols:
        copy.wait_recv()
    square = None
    for v in range(3):
        at = pl.ds(v * R, R)
        across = jnp.where(
            even, pltpu.roll(col_ahead[at, :], C - 1, 1), pltpu.roll(col_behind[at, :], 1, 1)
        )
        jump = across - col_own[at, :]
        square = jump * jump if square is None else square + jump * jump
    square = square + pltpu.roll(square, C // 2, 1)
    geo_b = chord_ghost[:, D : D + 1] * chord_live_b[:, :1]
    w_col[...] = square * jnp.where(even, wide(chord_geo[:, C - 1 :]), wide(geo_b))
    geo_ahead = jnp.broadcast_to(span_geo[R - 1 :, :], (8, C))
    geo_behind = jnp.broadcast_to(coef_span[pl.ds(D, 1), :] * span_live_b[:1, :], (8, C))

    def load_step(j, packed):
        edge = pltpu.roll(w_col[...], C - 1 - 2 * j, 1)
        w_s = jnp.where(row == R - 1, wide(w_ahead[pl.ds(j, 1), :]), ts[tile(j), :])
        w_c = jnp.where(lane == C - 1, edge, tc[tile(j), :])
        w_sb = jnp.where(row == 0, wide(w_behind[pl.ds(j, 1), :]), pltpu.roll(w_s, 1, 0))
        w_cb = jnp.where(lane == 0, edge, pltpu.roll(w_c, 1, 1))
        load = [
            (ssb[c] * w_sb - ss[c] * w_s) + (csb[c] * w_cb - cs[c] * w_c) for c in range(D)
        ]
        first_z = solve(load)
        keep(r0, j, load)
        keep(z0, j, first_z)
        values = dots(first_z)
        keep_dots(j, values)
        return pack_dots(j, values, packed)

    got_first = []
    for g in range(GROUPS):
        for b in range(GM // 8):
            block = g * (GM // 8) + b
            for copy in got_rows[block]:
                copy.wait_recv()
            to_ahead, to_behind = [], []
            for c in range(D):
                at = pl.ds((block * D + c) * 8, 8)
                jump = from_ahead[at, :] - row_last[at, :]
                to_ahead.append(jump * jump)
                jump = row_first[at, :] - from_behind[at, :]
                to_behind.append(jump * jump)
            w_ahead[pl.ds(block * 8, 8), :] = total_of(to_ahead) * geo_ahead
            w_behind[pl.ds(block * 8, 8), :] = total_of(to_behind) * geo_behind
        got_first.append(send_dots(0, g, over_group(g, load_step, zero)))

    for c in range(D):
        edge_s[c] = jnp.where(row == R - 1, ss[c], jnp.where(row == 0, ssb[c], 0.0))
        edge_c[c] = jnp.where(lane == C - 1, cs[c], jnp.where(lane == 0, csb[c], 0.0))
    for source, target in ((edge_s, back_s), (edge_c, back_c)):
        for c, value in enumerate(solve([source[c] for c in range(D)])):
            target[c] = value
    for n, source in enumerate((back_s, back_c)):
        for k, value in enumerate(dots([source[c] for c in range(D)])):
            cross[2 * k + n] = value

    def base_step(j, carry):
        z = of_mode(z0, j)
        image = operate(z, kept_dots(j))
        second = solve([a - b for a, b in zip(of_mode(r0, j), image)])
        keep(q0, j, image)
        keep(d0, j, second)
        keep_dots(j, dots(second))
        return carry

    for g in range(GROUPS):
        over_group(g, base_step, 0)
    widen(0)
    widen(1)

    def first_step(edge, j, packed):
        along_s, along_c = arrived(0, j, edge)
        values = [
            value + (cross[2 * k] * along_s + cross[2 * k + 1] * along_c)
            for k, value in enumerate(kept_dots(j))
        ]
        keep_dots(j, values)
        return pack_dots(j, values, packed)

    got_second = []
    for g in range(GROUPS):
        for copy in got_first[g]:
            copy.wait_recv()
        packed = over_group(g, functools.partial(first_step, edges_of(0, g)), zero)
        got_second.append(send_dots(1, g, packed))

    def finish_step(j, carry):
        along_s, along_c = hs[tile(j), :], hc[tile(j), :]
        z, image, second = of_mode(z0, j), of_mode(q0, j), of_mode(d0, j)
        image = [
            value - (edge_s[c] * along_s + edge_c[c] * along_c) for c, value in enumerate(image)
        ]
        second = [
            value + (back_s[c] * along_s + back_c[c] * along_c) for c, value in enumerate(second)
        ]
        left_over = [a - b for a, b in zip(of_mode(r0, j), image)]
        keep(q0, j, image)
        keep(d0, j, second)
        prod[tile(j), :] = total_of(a * b for a, b in zip(z, image))
        prod[tile(M + j), :] = total_of(a * b for a, b in zip(z, left_over))
        prod[tile(2 * M + j), :] = total_of(a * b for a, b in zip(second, left_over))
        image = operate(second, kept_dots(j))
        keep(image2, j, image)
        prod[tile(3 * M + j), :] = total_of(a * b for a, b in zip(second, image))
        return carry

    for g in range(GROUPS):
        over_group(g, finish_step, 0)

    def fold(k):
        rows = [prod[pl.ds(k * 8 * R + n, 8, stride=R), :] for n in range(R)]
        flip[pl.ds(k * 8, 8), :] = total_of(rows)

    for k in range(3 * M // 8):
        fold(k)
    widen(0)

    def second_step(edge, j, carry):
        along_s, along_c = arrived(1, j, edge)
        t_s, u_s, t_c, u_c = kept_dots(j)
        change = jnp.where(row == R - 1, t_s, jnp.where(row == 0, u_s, 0.0)) * along_s
        change = change + (
            jnp.where(lane == C - 1, t_c, jnp.where(lane == 0, u_c, 0.0)) * along_c
        )
        prod[tile(3 * M + j), :] = prod[tile(3 * M + j), :] - change
        return carry

    for g in range(GROUPS):
        for copy in got_second[g]:
            copy.wait_recv()
        over_group(g, functools.partial(second_step, edges_of(1, g)), 0)
    for k in range(3 * M // 8, 4 * M // 8):
        fold(k)

    def last_image(j, carry):
        along_s, along_c = hs[tile(j), :], hc[tile(j), :]
        for c in range(D):
            at = tile(j * D + c)
            image2[at, :] = image2[at, :] - (edge_s[c] * along_s + edge_c[c] * along_c)
        return carry

    widen(0)
    own = jnp.sum(jnp.transpose(flip[...]), axis=0, keepdims=True)
    for part, group in zip(parts, partners):
        members = len(group) + 1
        if part is not parts[0]:
            widen(1)
        part[pl.ds(0, 1), :] = own
        copies = [
            send(part.at[pl.ds(0, 1)], part.at[pl.ds(n + 1, 1)], device)
            for n, device in enumerate(group)
        ]
        if part is parts[0]:
            for g in range(GROUPS):
                over_group(g, last_image, 0)
        for copy in copies:
            copy.wait_recv()
        own = jnp.sum(part[pl.ds(0, members), :], axis=0, keepdims=True)

    zq = wide(own)
    zs = pltpu.roll(zq, C - M, 1)
    ds = pltpu.roll(zq, C - 2 * M, 1)
    dv = pltpu.roll(zq, C - 3 * M, 1)
    dq = zs - ds
    ratio = dq / zq
    second_part = (ds - dq * (zs / zq)) / (dv - ratio * dq)
    excess = (zs - dq * second_part) / zq

    def spread(j, carry):
        over[tile(j), :] = wide(pltpu.roll(excess, C - 1 - j, 1)[:, C - 1 :])
        other[tile(j), :] = wide(pltpu.roll(second_part, C - 1 - j, 1)[:, C - 1 :])
        return carry

    for g in range(GROUPS):
        over_group(g, spread, 0)
    for copy in sent:
        copy.wait_send()


def body(n_slab, n_sub, mode_shapes, span_stiff, chord_stiff, span_geo, chord_geo, ground, chord_len):
    stages = digit_stages(n_slab, n_sub)
    f32 = jnp.float32
    members = []
    for digits in stages:
        total = 1
        for _, _, size in digits:
            total *= size
        members.append(total)
    n_sends = 4 + 2 * (M // 8) + 8 * GROUPS + sum(members) - len(members)

    def big():
        return pltpu.VMEM((M * D * R, C), f32)

    rows = M * D
    scratch = [
        pltpu.SMEM(chord_len.shape, jnp.int32),
        pltpu.VMEM((M, D, R, C), jnp.bfloat16),
        pltpu.VMEM((D, R, C), f32),
        pltpu.VMEM((D, R, C), f32),
        pltpu.VMEM((R, C), f32),
        pltpu.VMEM((R, C), f32),
        pltpu.VMEM((D, R, C), f32),
        big(),
        pltpu.VMEM((D, R, C), f32),
        pltpu.VMEM((D, R, C), f32),
        pltpu.VMEM((D, R, C), f32),
        pltpu.VMEM((D, R, C), f32),
        pltpu.VMEM((D, R, C), f32),
        pltpu.VMEM((D, R, C), f32),
        pltpu.VMEM((8, R, C), f32),
        pltpu.VMEM((M * R, C), f32),
        pltpu.VMEM((M * R, C), f32),
        pltpu.VMEM((21, R, C), f32),
        pltpu.VMEM((M * R, C), f32),
        pltpu.VMEM((M * R, C), f32),
        pltpu.VMEM((M * R, C), f32),
        pltpu.VMEM((M * R, C), f32),
        pltpu.VMEM((4 * M * R, C), f32),
        pltpu.VMEM((4 * M, C), f32),
        pltpu.VMEM((2, R, C), f32),
        pltpu.VMEM((R, C), f32),
        pltpu.VMEM((R, C), f32),
        pltpu.VMEM((rows, C), f32),
        pltpu.VMEM((rows, C), f32),
        pltpu.VMEM((rows, C), f32),
        pltpu.VMEM((rows, C), f32),
        pltpu.VMEM((3 * R, C), f32),
        pltpu.VMEM((3 * R, C), f32),
        pltpu.VMEM((3 * R, C), f32),
        pltpu.VMEM((M, C), f32),
        pltpu.VMEM((M, C), f32),
        pltpu.VMEM((R, C), f32),
        pltpu.VMEM((2 * M, C), f32),
        pltpu.VMEM((2 * M, C), f32),
        pltpu.VMEM((2 * M, C), f32),
        pltpu.VMEM((2 * M, C), f32),
        pltpu.VMEM((2, GROUPS, R, C), f32),
        pltpu.VMEM((2, GROUPS, R, C), f32),
        pltpu.VMEM((2, GROUPS, R, C), f32),
    ]
    scratch += [pltpu.VMEM((max(8, n), C), f32) for n in members]
    scratch += [
        pltpu.SemaphoreType.DMA((7,)),
        pltpu.SemaphoreType.DMA((n_sends,)),
        pltpu.SemaphoreType.DMA((n_sends,)),
        pltpu.SemaphoreType.REGULAR((2, 4)),
    ]
    operands = [
        pltpu.with_memory_space_constraint(value, pltpu.HBM)
        for value in (
            mode_shapes, span_stiff, chord_stiff, span_geo, chord_geo, ground, chord_len
        )
    ]
    in_hbm = pl.BlockSpec(memory_space=pltpu.HBM)
    shape = jax.ShapeDtypeStruct((M * D * R, C), f32)
    per_mode = jax.ShapeDtypeStruct((M * R, C), f32)
    in_vmem = pl.BlockSpec(memory_space=pltpu.VMEM)
    fields = pl.pallas_call(
        functools.partial(kernel, n_slab, n_sub, stages),
        out_shape=(shape,) * 5 + (per_mode,) * 2,
        in_specs=[in_hbm] * 7,
        out_specs=(in_vmem,) * 7,
        scratch_shapes=scratch,
        compiler_params=pltpu.CompilerParams(
            collective_id=0, has_side_effects=True, vmem_limit_bytes=24 << 20
        ),
    )(*operands)
    full = (M, D, R, C)
    r0, z0, q0, d0, image2 = [value.reshape(full) for value in fields[:5]]
    over, other = [value.reshape(M, 1, R, C) for value in fields[5:]]
    return z0 + over * z0 + other * d0, (r0 - q0) - over * q0 - other * image2


def solution(mesh):
    sizes = (mesh.shape["slab"], mesh.shape["sub"])
    return jax.shard_map(
        functools.partial(body, *sizes),
        mesh=mesh,
        in_specs=(
            P(None, None, "slab", "sub"),
            P(None, "slab", "sub"),
            P(None, "slab", "sub"),
            P("slab", "sub"),
            P("slab", "sub"),
            P(None, "slab", "sub"),
            P(),
        ),
        out_specs=(P(None, None, "slab", "sub"), P(None, None, "slab", "sub")),
        check_vma=False,
    )
```

```python
import functools

import jax
import jax.numpy as jnp
from jax import lax
from jax.experimental import pallas as pl
from jax.experimental.pallas import tpu as pltpu
from jax.sharding import PartitionSpec as P

MESH = pl.DeviceIdType.MESH
D = 6
R, C = 8, 128
M = 32
GROUPS = 2
GM = M // GROUPS
UNROLL = 16


def digits_of(n_slab):
    core = 2
    z = 16 if n_slab % 32 == 0 else 4 if n_slab % 8 == 0 else 1
    return core, z, n_slab // (core * z)


def digit_stages(n_slab, n_sub):
    core, z, y = digits_of(n_slab)
    return [[("slab", 1, core), ("sub", 1, n_sub), ("slab", core * z, y)], [("slab", core, z)]]


def stage_partners(digits, slab, sub):
    total = 1
    for _, _, size in digits:
        total *= size
    partners = []
    for offset in range(1, total):
        rest, at = offset, {"slab": slab, "sub": sub}
        for axis, stride, size in digits:
            step, rest = rest % size, rest // size
            digit = (at[axis] // stride) % size
            at[axis] = at[axis] + ((digit + step) % size - digit) * stride
        partners.append((at["slab"], at["sub"]))
    return partners


def farthest_first(digits):
    total = 1
    for _, _, size in digits:
        total *= size

    def hops(offset):
        way, rest = 0, offset + 1
        for axis, stride, size in digits:
            step, rest = rest % size, rest // size
            if (axis, stride) != ("slab", 1):
                way += min(step, size - step)
        return way

    return sorted(range(total - 1), key=lambda offset: -hops(offset))


def total_of(terms):
    terms = list(terms)
    while len(terms) > 1:
        terms = [sum(terms[i : i + 2][1:], terms[i]) for i in range(0, len(terms), 2)]
    return terms[0]


def place(i, j):
    i, j = min(i, j), max(i, j)
    return i * D - i * (i - 1) // 2 + j - i


def kernel(
    n_slab,
    n_sub,
    stages,
    m_any,
    ss_any,
    cs_any,
    sg_any,
    cg_any,
    gr_any,
    len_any,
    r0,
    z0,
    q0,
    d0,
    image2,
    over,
    other,
    len_ref,
    m_in,
    ss,
    cs,
    sg,
    cg,
    gr,
    field,
    ssb,
    csb,
    edge_s,
    edge_c,
    back_s,
    back_c,
    cross,
    hs,
    hc,
    fac,
    ts,
    us,
    tc,
    uc,
    prod,
    flip,
    coef_send,
    coef_span,
    coef_chord,
    row_first,
    row_last,
    from_ahead,
    from_behind,
    col_own,
    col_ahead,
    col_behind,
    w_ahead,
    w_behind,
    w_col,
    t_send,
    u_send,
    u_ahead,
    t_behind,
    tu_send,
    tu_ahead,
    tu_behind,
    *rest,
):
    parts = rest[: len(stages)]
    in_sem, send_sem, recv_sem, here_sem = rest[len(stages) :]
    slab, sub = lax.axis_index("slab"), lax.axis_index("sub")
    ahead = (lax.rem(slab + 1, n_slab), sub)
    behind = (lax.rem(slab + n_slab - 1, n_slab), sub)
    right = (slab, lax.rem(sub + 1, n_sub))
    left = (slab, lax.rem(sub + n_sub - 1, n_sub))
    partners = [stage_partners(digits, slab, sub) for digits in stages]

    loads = []
    for k, (source, target) in enumerate(
        ((m_any, m_in), (ss_any, ss), (cs_any, cs), (sg_any, sg), (cg_any, cg), (gr_any, gr), (len_any, len_ref))
    ):
        copy = pltpu.make_async_copy(source, target, in_sem.at[k])
        loads.append(copy)

    core, z_size, y_size = digits_of(n_slab)
    ring_x = stage_partners([("sub", 1, n_sub)], slab, sub)
    ring_y = stage_partners([("slab", core * z_size, y_size)], slab, sub)
    ring_z = stage_partners([("slab", core, z_size)], slab, sub)
    twin = stage_partners([("slab", 1, core)], slab, sub)

    def both_ways(ring, distance):
        return [ring[distance - 1], ring[len(ring) - distance]] if ring else []

    def tell(semaphore, devices):
        for device in devices:
            pl.semaphore_signal(semaphore, inc=1, device_id=device, device_id_type=MESH)

    barrier = pltpu.get_barrier_semaphore()
    greeted = [ahead, behind] + both_ways(ring_x, 1) + twin
    greeted += both_ways(ring_y, 1) + both_ways(ring_z, 1)
    tell(barrier, greeted)
    for copy in loads:
        copy.start()

    steps = [
        [both_ways(ring_x, 1), both_ways(ring_y, 1), both_ways(ring_y, 1), twin],
        [both_ways(ring_z, distance) for distance in (1, 2, 4) if 2 * distance < z_size],
    ]
    told = [0, 0]

    def widen(n):
        chain, step = steps[n], told[n]
        if 0 < step <= len(chain) and chain[step - 1]:
            pl.semaphore_wait(here_sem.at[n, step - 1], len(chain[step - 1]))
        if step < len(chain):
            tell(here_sem.at[n, step], chain[step])
        told[n] += 1

    row = lax.broadcasted_iota(jnp.int32, (R, C), 0)
    lane = lax.broadcasted_iota(jnp.int32, (R, C), 1)
    pair = lax.shift_right_logical(lane, 1)
    even = lane - 2 * pair == 0

    def tile(k):
        return pl.ds(pl.multiple_of(k * R, R), R)

    def wide(value):
        return jnp.broadcast_to(value, (R, C))

    def of_mode(ref, j):
        return [ref[tile(j * D + c), :] for c in range(D)]

    def keep(ref, j, vector):
        for c in range(D):
            ref[tile(j * D + c), :] = vector[c]

    def over_group(g, step, carry):
        def some(i, carry):
            for u in range(UNROLL):
                carry = step(g * GM + i * UNROLL + u, carry)
            return carry

        return lax.fori_loop(0, GM // UNROLL, some, carry)

    sent = []
    count = [0]

    def send(source, target, device):
        k = count[0]
        count[0] += 1
        copy = pltpu.make_async_remote_copy(
            src_ref=source,
            dst_ref=target,
            send_sem=send_sem.at[k],
            recv_sem=recv_sem.at[k],
            device_id=device,
            device_id_type=MESH,
        )
        copy.start()
        sent.append(copy)
        return copy

    loads[0].wait()

    def pack(i, packs):
        packs = list(packs)
        for u in range(UNROLL):
            j = i * UNROLL + u
            for c in range(D):
                value = m_in[j, c].astype(jnp.float32)
                field[tile(j * D + c), :] = value
                half = 32 * (c % 2)
                turned = pltpu.roll(value, 2 * (j + half) + 1, 1)
                packs[c // 2] = jnp.where(pair == j + half, turned, packs[c // 2])
        return tuple(packs)

    zero = jnp.zeros((R, C), jnp.float32)
    packs = lax.fori_loop(0, M // UNROLL, pack, (zero,) * 3)
    for v in range(3):
        col_own[pl.ds(v * R, R), :] = packs[v]
    for g in range(M // 8):
        for c in range(D):
            at = pl.ds((g * D + c) * 8, 8)
            row_first[at, :] = field[pl.ds((g * 8 * D + c) * R, 8, stride=D * R), :]
            row_last[at, :] = field[pl.ds((g * 8 * D + c) * R + R - 1, 8, stride=D * R), :]

    for copy in loads[1:]:
        copy.wait()
    span_coef, chord_coef = zero, zero
    for c in range(D + 1):
        mine = ss[c] if c < D else sg[...]
        span_coef = jnp.where(row == c, wide(mine[R - 1 :, :]), span_coef)
        mine = cs[c] if c < D else cg[...]
        chord_coef = jnp.where(lane == c, wide(mine[:, C - 1 :]), chord_coef)
    coef_send[0] = span_coef
    coef_send[1] = chord_coef

    pl.semaphore_wait(barrier, len(greeted))
    widen(0)
    widen(1)
    got_coef = [
        send(coef_send.at[0], coef_span, ahead),
        send(coef_send.at[1], coef_chord, right),
    ]
    got_cols = [send(col_own, col_behind, right), send(col_own, col_ahead, left)]
    got_rows = []
    for g in range(M // 8):
        at = pl.ds(g * 8 * D, 8 * D)
        got_rows.append(
            [
                send(row_last.at[at], from_behind.at[at], ahead),
                send(row_first.at[at], from_ahead.at[at], behind),
            ]
        )

    n_stations = n_slab * R
    first = slab * R
    length = jnp.zeros((R, C), jnp.int32)
    length_next = jnp.zeros((R, C), jnp.int32)
    length_prev = jnp.zeros((R, C), jnp.int32)
    for k in range(-1, R + 1):
        here = len_ref[jnp.clip(first + k, 0, n_stations - 1)]
        if 0 <= k < R:
            length = jnp.where(row == k, here, length)
        if k >= 1:
            length_next = jnp.where(row == k - 1, here, length_next)
        if k < R - 1:
            length_prev = jnp.where(row == k + 1, here, length_prev)
    column = lane + sub * C
    station = row + first
    one = jnp.ones((R, C), jnp.float32)
    span_live = jnp.where(
        (column < length) & (column < length_next) & (station < n_stations - 1), one, zero
    )
    span_live_b = jnp.where(
        (column < length) & (column < length_prev) & (station > 0), one, zero
    )
    chord_live = jnp.where(column + 1 < length, one, zero)
    chord_live_b = jnp.where((column < length) & (column > 0), one, zero)
    span_geo = sg[...] * span_live
    chord_geo = cg[...] * chord_live

    sg[...] = span_geo
    cg[...] = chord_geo

    def weigh(j, carry):
        modes = of_mode(field, j)
        jumps = [pltpu.roll(value, R - 1, 0) - value for value in modes]
        ts[tile(j), :] = total_of(jump * jump for jump in jumps) * sg[...]
        jumps = [pltpu.roll(value, C - 1, 1) - value for value in modes]
        tc[tile(j), :] = total_of(jump * jump for jump in jumps) * cg[...]
        return carry

    for g in range(GROUPS):
        over_group(g, weigh, 0)

    for copy in got_coef:
        copy.wait_recv()
    widen(0)
    widen(1)
    chord_ghost = coef_chord[...]
    for c in range(D):
        mine = ss[c]
        back = jnp.where(row == 0, wide(coef_span[pl.ds(c, 1), :]), pltpu.roll(mine, 1, 0))
        ssb[c] = back * span_live_b
        ss[c] = mine * span_live
        mine = cs[c]
        back = jnp.where(lane == 0, wide(chord_ghost[:, c : c + 1]), pltpu.roll(mine, 1, 1))
        csb[c] = back * chord_live_b
        cs[c] = mine * chord_live
    a_s = [ss[c] for c in range(D)]
    a_c = [cs[c] for c in range(D)]
    b_s = [ssb[c] for c in range(D)]
    b_c = [csb[c] for c in range(D)]
    low = [[None] * D for _ in range(D)]
    raw = [[None] * D for _ in range(D)]
    inverse = []
    for j in range(D):
        for i in range(j, D):
            entry = (a_s[i] * a_s[j] + b_s[i] * b_s[j]) + (a_c[i] * a_c[j] + b_c[i] * b_c[j])
            if i == j:
                entry = entry + gr[i]
            for n in range(j):
                entry = entry - raw[i][n] * low[j][n]
            raw[i][j] = entry
        inverse.append(1.0 / raw[j][j])
        for i in range(j + 1, D):
            low[i][j] = raw[i][j] * inverse[j]
    unit = [[None] * D for _ in range(D)]
    for j in range(D):
        for i in range(j + 1, D):
            entry = low[i][j]
            for n in range(j + 1, i):
                entry = entry + low[i][n] * unit[n][j]
            unit[i][j] = -entry
    scaled = [[None] * D for _ in range(D)]
    for k in range(D):
        for i in range(k):
            scaled[k][i] = unit[k][i] * inverse[k]
        scaled[k][k] = inverse[k]
    for i in range(D):
        for j in range(i, D):
            terms = [scaled[j][i] if i < j else inverse[j]]
            terms += [scaled[k][i] * unit[k][j] for k in range(j + 1, D)]
            fac[place(i, j)] = total_of(terms)

    def solve(vector):
        return [total_of(fac[place(i, j)] * vector[j] for j in range(D)) for i in range(D)]

    def dots(vector):
        return [
            total_of(coef[c] * vector[c] for c in range(D)) for coef in (ss, ssb, cs, csb)
        ]

    def keep_dots(j, values):
        for ref, value in zip((ts, us, tc, uc), values):
            ref[tile(j), :] = value

    def kept_dots(j):
        return [ref[tile(j), :] for ref in (ts, us, tc, uc)]

    def pack_dots(j, values, packed):
        turned = pltpu.roll(jnp.where(lane == 0, values[3], values[2]), 2 * j + 1, 1)
        return jnp.where(pair == j, turned, packed)

    def send_dots(turn, g, packed):
        at = pl.ds(turn * M + g * GM, GM)
        for b in range(GM // 8):
            from_mode = g * GM + b * 8
            to = pl.ds(turn * M + from_mode, 8)
            t_send[to, :] = ts[pl.ds(from_mode * R + R - 1, 8, stride=R), :]
            u_send[to, :] = us[pl.ds(from_mode * R, 8, stride=R), :]
        tu_send[turn, g] = packed
        return [
            send(t_send.at[at], t_behind.at[at], ahead),
            send(u_send.at[at], u_ahead.at[at], behind),
            send(tu_send.at[turn, g], tu_behind.at[turn, g], right),
            send(tu_send.at[turn, g], tu_ahead.at[turn, g], left),
        ]

    def edges_of(turn, g):
        return jnp.where(
            even,
            pltpu.roll(tu_ahead[turn, g], C - 1, 1),
            pltpu.roll(tu_behind[turn, g], 1, 1),
        )

    def operate(vector, values):
        t_s, u_s, t_c, u_c = values
        u_s_next = jnp.where(row == R - 1, 0.0, pltpu.roll(u_s, R - 1, 0))
        t_s_prev = jnp.where(row == 0, 0.0, pltpu.roll(t_s, 1, 0))
        u_c_next = jnp.where(lane == C - 1, 0.0, pltpu.roll(u_c, C - 1, 1))
        t_c_prev = jnp.where(lane == 0, 0.0, pltpu.roll(t_c, 1, 1))
        e_s, e_sb = u_s_next - t_s, u_s - t_s_prev
        e_c, e_cb = u_c_next - t_c, u_c - t_c_prev
        return [
            (gr[c] * vector[c] + (ssb[c] * e_sb - ss[c] * e_s)) + (csb[c] * e_cb - cs[c] * e_c)
            for c in range(D)
        ]

    def arrived(turn, j, edge):
        at = pl.ds(turn * M + j, 1)
        along_s = jnp.where(row == 0, wide(t_behind[at, :]), wide(u_ahead[at, :]))
        along_c = pltpu.roll(edge, C - 1 - 2 * j, 1)
        hs[tile(j), :] = along_s
        hc[tile(j), :] = along_c
        return along_s, along_c

    for copy in got_cols:
        copy.wait_recv()
    square = None
    for v in range(3):
        at = pl.ds(v * R, R)
        across = jnp.where(
            even, pltpu.roll(col_ahead[at, :], C - 1, 1), pltpu.roll(col_behind[at, :], 1, 1)
        )
        jump = across - col_own[at, :]
        square = jump * jump if square is None else square + jump * jump
    square = square + pltpu.roll(square, C // 2, 1)
    geo_b = chord_ghost[:, D : D + 1] * chord_live_b[:, :1]
    w_col[...] = square * jnp.where(even, wide(chord_geo[:, C - 1 :]), wide(geo_b))
    geo_ahead = jnp.broadcast_to(span_geo[R - 1 :, :], (8, C))
    geo_behind = jnp.broadcast_to(coef_span[pl.ds(D, 1), :] * span_live_b[:1, :], (8, C))

    def load_step(j, packed):
        edge = pltpu.roll(w_col[...], C - 1 - 2 * j, 1)
        w_s = jnp.where(row == R - 1, wide(w_ahead[pl.ds(j, 1), :]), ts[tile(j), :])
        w_c = jnp.where(lane == C - 1, edge, tc[tile(j), :])
        w_sb = jnp.where(row == 0, wide(w_behind[pl.ds(j, 1), :]), pltpu.roll(w_s, 1, 0))
        w_cb = jnp.where(lane == 0, edge, pltpu.roll(w_c, 1, 1))
        load = [
            (ssb[c] * w_sb - ss[c] * w_s) + (csb[c] * w_cb - cs[c] * w_c) for c in range(D)
        ]
        first_z = solve(load)
        keep(r0, j, load)
        keep(z0, j, first_z)
        values = dots(first_z)
        keep_dots(j, values)
        return pack_dots(j, values, packed)

    got_first = []
    for g in range(GROUPS):
        for b in range(GM // 8):
            block = g * (GM // 8) + b
            for copy in got_rows[block]:
                copy.wait_recv()
            to_ahead, to_behind = [], []
            for c in range(D):
                at = pl.ds((block * D + c) * 8, 8)
                jump = from_ahead[at, :] - row_last[at, :]
                to_ahead.append(jump * jump)
                jump = row_first[at, :] - from_behind[at, :]
                to_behind.append(jump * jump)
            w_ahead[pl.ds(block * 8, 8), :] = total_of(to_ahead) * geo_ahead
            w_behind[pl.ds(block * 8, 8), :] = total_of(to_behind) * geo_behind
        got_first.append(send_dots(0, g, over_group(g, load_step, zero)))

    for c in range(D):
        edge_s[c] = jnp.where(row == R - 1, ss[c], jnp.where(row == 0, ssb[c], 0.0))
        edge_c[c] = jnp.where(lane == C - 1, cs[c], jnp.where(lane == 0, csb[c], 0.0))
    for source, target in ((edge_s, back_s), (edge_c, back_c)):
        for c, value in enumerate(solve([source[c] for c in range(D)])):
            target[c] = value
    for n, source in enumerate((back_s, back_c)):
        for k, value in enumerate(dots([source[c] for c in range(D)])):
            cross[2 * k + n] = value

    def base_step(j, carry):
        z = of_mode(z0, j)
        image = operate(z, kept_dots(j))
        second = solve([a - b for a, b in zip(of_mode(r0, j), image)])
        keep(q0, j, image)
        keep(d0, j, second)
        keep_dots(j, dots(second))
        return carry

    for g in range(GROUPS):
        over_group(g, base_step, 0)
    widen(0)
    widen(1)

    def first_step(edge, j, packed):
        along_s, along_c = arrived(0, j, edge)
        values = [
            value + (cross[2 * k] * along_s + cross[2 * k + 1] * along_c)
            for k, value in enumerate(kept_dots(j))
        ]
        keep_dots(j, values)
        return pack_dots(j, values, packed)

    got_second = []
    for g in range(GROUPS):
        for copy in got_first[g]:
            copy.wait_recv()
        packed = over_group(g, functools.partial(first_step, edges_of(0, g)), zero)
        got_second.append(send_dots(1, g, packed))

    def finish_step(j, carry):
        along_s, along_c = hs[tile(j), :], hc[tile(j), :]
        z, image, second = of_mode(z0, j), of_mode(q0, j), of_mode(d0, j)
        image = [
            value - (edge_s[c] * along_s + edge_c[c] * along_c) for c, value in enumerate(image)
        ]
        second = [
            value + (back_s[c] * along_s + back_c[c] * along_c) for c, value in enumerate(second)
        ]
        left_over = [a - b for a, b in zip(of_mode(r0, j), image)]
        keep(q0, j, image)
        keep(d0, j, second)
        prod[tile(j), :] = total_of(a * b for a, b in zip(z, image))
        prod[tile(M + j), :] = total_of(a * b for a, b in zip(z, left_over))
        prod[tile(2 * M + j), :] = total_of(a * b for a, b in zip(second, left_over))
        image = operate(second, kept_dots(j))
        keep(image2, j, image)
        prod[tile(3 * M + j), :] = total_of(a * b for a, b in zip(second, image))
        return carry

    for g in range(GROUPS):
        over_group(g, finish_step, 0)

    def fold(k):
        rows = [prod[pl.ds(k * 8 * R + n, 8, stride=R), :] for n in range(R)]
        flip[pl.ds(k * 8, 8), :] = total_of(rows)

    for k in range(3 * M // 8):
        fold(k)
    widen(0)

    def second_step(edge, j, carry):
        along_s, along_c = arrived(1, j, edge)
        t_s, u_s, t_c, u_c = kept_dots(j)
        change = jnp.where(row == R - 1, t_s, jnp.where(row == 0, u_s, 0.0)) * along_s
        change = change + (
            jnp.where(lane == C - 1, t_c, jnp.where(lane == 0, u_c, 0.0)) * along_c
        )
        prod[tile(3 * M + j), :] = prod[tile(3 * M + j), :] - change
        return carry

    for g in range(GROUPS):
        for copy in got_second[g]:
            copy.wait_recv()
        over_group(g, functools.partial(second_step, edges_of(1, g)), 0)
    for k in range(3 * M // 8, 4 * M // 8):
        fold(k)

    def last_image(j, carry):
        along_s, along_c = hs[tile(j), :], hc[tile(j), :]
        for c in range(D):
            at = tile(j * D + c)
            image2[at, :] = image2[at, :] - (edge_s[c] * along_s + edge_c[c] * along_c)
        return carry

    widen(0)
    own = jnp.sum(jnp.transpose(flip[...]), axis=0, keepdims=True)
    for part, group, digits in zip(parts, partners, stages):
        members = len(group) + 1
        if part is not parts[0]:
            widen(1)
        part[pl.ds(0, 1), :] = own
        copies = [
            send(part.at[pl.ds(0, 1)], part.at[pl.ds(n + 1, 1)], group[n])
            for n in farthest_first(digits)
        ]
        if part is parts[0]:
            for g in range(GROUPS):
                over_group(g, last_image, 0)
        for copy in copies:
            copy.wait_recv()
        own = jnp.sum(part[pl.ds(0, members), :], axis=0, keepdims=True)

    zq = wide(own)
    zs = pltpu.roll(zq, C - M, 1)
    ds = pltpu.roll(zq, C - 2 * M, 1)
    dv = pltpu.roll(zq, C - 3 * M, 1)
    dq = zs - ds
    ratio = dq / zq
    second_part = (ds - dq * (zs / zq)) / (dv - ratio * dq)
    excess = (zs - dq * second_part) / zq

    def spread(j, carry):
        over[tile(j), :] = wide(pltpu.roll(excess, C - 1 - j, 1)[:, C - 1 :])
        other[tile(j), :] = wide(pltpu.roll(second_part, C - 1 - j, 1)[:, C - 1 :])
        return carry

    for g in range(GROUPS):
        over_group(g, spread, 0)
    for copy in sent:
        copy.wait_send()


def body(n_slab, n_sub, mode_shapes, span_stiff, chord_stiff, span_geo, chord_geo, ground, chord_len):
    stages = digit_stages(n_slab, n_sub)
    f32 = jnp.float32
    members = []
    for digits in stages:
        total = 1
        for _, _, size in digits:
            total *= size
        members.append(total)
    n_sends = 4 + 2 * (M // 8) + 8 * GROUPS + sum(members) - len(members)

    def big():
        return pltpu.VMEM((M * D * R, C), f32)

    rows = M * D
    scratch = [
        pltpu.SMEM(chord_len.shape, jnp.int32),
        pltpu.VMEM((M, D, R, C), jnp.bfloat16),
        pltpu.VMEM((D, R, C), f32),
        pltpu.VMEM((D, R, C), f32),
        pltpu.VMEM((R, C), f32),
        pltpu.VMEM((R, C), f32),
        pltpu.VMEM((D, R, C), f32),
        big(),
        pltpu.VMEM((D, R, C), f32),
        pltpu.VMEM((D, R, C), f32),
        pltpu.VMEM((D, R, C), f32),
        pltpu.VMEM((D, R, C), f32),
        pltpu.VMEM((D, R, C), f32),
        pltpu.VMEM((D, R, C), f32),
        pltpu.VMEM((8, R, C), f32),
        pltpu.VMEM((M * R, C), f32),
        pltpu.VMEM((M * R, C), f32),
        pltpu.VMEM((21, R, C), f32),
        pltpu.VMEM((M * R, C), f32),
        pltpu.VMEM((M * R, C), f32),
        pltpu.VMEM((M * R, C), f32),
        pltpu.VMEM((M * R, C), f32),
        pltpu.VMEM((4 * M * R, C), f32),
        pltpu.VMEM((4 * M, C), f32),
        pltpu.VMEM((2, R, C), f32),
        pltpu.VMEM((R, C), f32),
        pltpu.VMEM((R, C), f32),
        pltpu.VMEM((rows, C), f32),
        pltpu.VMEM((rows, C), f32),
        pltpu.VMEM((rows, C), f32),
        pltpu.VMEM((rows, C), f32),
        pltpu.VMEM((3 * R, C), f32),
        pltpu.VMEM((3 * R, C), f32),
        pltpu.VMEM((3 * R, C), f32),
        pltpu.VMEM((M, C), f32),
        pltpu.VMEM((M, C), f32),
        pltpu.VMEM((R, C), f32),
        pltpu.VMEM((2 * M, C), f32),
        pltpu.VMEM((2 * M, C), f32),
        pltpu.VMEM((2 * M, C), f32),
        pltpu.VMEM((2 * M, C), f32),
        pltpu.VMEM((2, GROUPS, R, C), f32),
        pltpu.VMEM((2, GROUPS, R, C), f32),
        pltpu.VMEM((2, GROUPS, R, C), f32),
    ]
    scratch += [pltpu.VMEM((max(8, n), C), f32) for n in members]
    scratch += [
        pltpu.SemaphoreType.DMA((7,)),
        pltpu.SemaphoreType.DMA((n_sends,)),
        pltpu.SemaphoreType.DMA((n_sends,)),
        pltpu.SemaphoreType.REGULAR((2, 4)),
    ]
    operands = [
        pltpu.with_memory_space_constraint(value, pltpu.HBM)
        for value in (
            mode_shapes, span_stiff, chord_stiff, span_geo, chord_geo, ground, chord_len
        )
    ]
    in_hbm = pl.BlockSpec(memory_space=pltpu.HBM)
    shape = jax.ShapeDtypeStruct((M * D * R, C), f32)
    per_mode = jax.ShapeDtypeStruct((M * R, C), f32)
    in_vmem = pl.BlockSpec(memory_space=pltpu.VMEM)
    fields = pl.pallas_call(
        functools.partial(kernel, n_slab, n_sub, stages),
        out_shape=(shape,) * 5 + (per_mode,) * 2,
        in_specs=[in_hbm] * 7,
        out_specs=(in_vmem,) * 7,
        scratch_shapes=scratch,
        compiler_params=pltpu.CompilerParams(
            collective_id=0, has_side_effects=True, vmem_limit_bytes=24 << 20
        ),
    )(*operands)
    full = (M, D, R, C)
    r0, z0, q0, d0, image2 = [value.reshape(full) for value in fields[:5]]
    over, other = [value.reshape(M, 1, R, C) for value in fields[5:]]
    return z0 + over * z0 + other * d0, (r0 - q0) - over * q0 - other * image2


def solution(mesh):
    sizes = (mesh.shape["slab"], mesh.shape["sub"])
    return jax.shard_map(
        functools.partial(body, *sizes),
        mesh=mesh,
        in_specs=(
            P(None, None, "slab", "sub"),
            P(None, "slab", "sub"),
            P(None, "slab", "sub"),
            P("slab", "sub"),
            P("slab", "sub"),
            P(None, "slab", "sub"),
            P(),
        ),
        out_specs=(P(None, None, "slab", "sub"), P(None, None, "slab", "sub")),
        check_vma=False,
    )
```
